32 devices in a mesh: gx: 8 (over z, x), gy: 4 (over y, core).
Axes of the slice: x: 2, y: 2, z: 4, core: 2. Of those that a mesh axis runs over, the one named last changes fastest.
Arguments:
- adjoint_block: float32 [4, 3, 64, 32, 512], P(None, None, None, 'gx', 'gy'), may hold values from -18 to 18
- base_flow: float32 [2, 3, 64, 32, 512], P(None, None, None, 'gx', 'gy'), may hold values from -4 to 4
- direct_modes: float32 [8, 3, 64, 32, 512], P(None, None, None, 'gx', 'gy'), may hold values from -0.0034179688 to 0.0034179688
- dual_modes: float32 [8, 3, 64, 32, 512], P(None, None, None, 'gx', 'gy'), may hold values from -0.6 to 0.6
Outputs:
- next_block: float32 [4, 3, 64, 32, 512], P(None, None, None, 'gx', 'gy')
- growth: float32 [4, 4], replicated
The draws below stay inside these ranges and needn't reach their ends.
All inputs are finite; a program needn't handle non-finite values.
Results may differ from the reference program's by a relative error of at most 0.0001.
Values sent between devices are 32-bit elements; how exact they have to be, the bound alone decides.
No kernel may reach another device: no remote copies, remote signals or barrier semaphores. Data moves between devices by JAX's collectives and lax.ppermute only.
A program may use at most 128 MiB of HBM per device.

```python
import math
import jax
import jax.numpy as jnp
from jax import lax

NZ = 64
VECS = 4
MODES = 8
NX = 32
NY = 512


def draw_adjoint_block(key, part):
    shape = (VECS, 3, NZ, NX, NY)
    ramp = 1.0 + 2.0 * jnp.arange(NX, dtype=jnp.float32) / max(NX - 1, 1)
    values = jax.random.truncated_normal(key, -6.0, 6.0, shape, jnp.float32)
    return values * ramp[:, None]


def block_levels(own_key, extent, cuts, least, high):
    level, own = 1.0, jax.random.fold_in(own_key, 6)
    for axis_at, shards_of in cuts:
        steps = jnp.exp(jax.random.uniform(jax.random.fold_in(own, axis_at), (shards_of,), jnp.float32, least / len(cuts), high / len(cuts)))
        level = level * jnp.repeat(steps, extent[axis_at] // shards_of).reshape([-1 if axis == axis_at else 1 for axis in range(len(extent))])
    return level


def bell_draw(rng, shape, width, most, shards=(), kind=jnp.bfloat16):
    factor_of = block_levels(rng, shape, shards, -0.22, 0.18) if shards else 1.0
    values = jax.random.normal(rng, shape, jnp.float32) * width * factor_of
    return jnp.minimum(jnp.maximum(values, -most), most).astype(kind)


def setup_inputs(seed: int = 0) -> dict:
    keys = jax.random.split(jax.random.key(seed), 5)
    return {
        "adjoint_block": draw_adjoint_block(jax.random.fold_in(keys[4], 71), 0),
        "base_flow": bell_draw(keys[1], (2, 3, NZ, NX, NY), 1.0, 4.0, ((3, 8), (4, 4)), jnp.float32),
        "direct_modes": bell_draw(keys[2], (MODES, 3, NZ, NX, NY), (3 * NZ * NX * NY) ** -0.5, 0.0034179688, ((3, 8), (4, 4)), jnp.float32),
        "dual_modes": bell_draw(keys[3], (MODES, 3, NZ, NX, NY), 0.1, 0.6, ((3, 8), (4, 4)), jnp.float32),
    }


step_size = 0.1
viscosity = 0.2

def central_x(padded):
    return 0.5 * (padded[..., 2:, 1:-1] - padded[..., :-2, 1:-1])

def central_y(padded):
    return 0.5 * (padded[..., 1:-1, 2:] - padded[..., 1:-1, :-2])

def central_z(interior):
    return 0.5 * (jnp.roll(interior, -1, axis=-3) - jnp.roll(interior, 1, axis=-3))

def laplace(padded):
    interior = padded[..., 1:-1, 1:-1]
    beside_all = padded[..., 2:, 1:-1] + padded[..., :-2, 1:-1] + padded[..., 1:-1, 2:] + padded[..., 1:-1, :-2]
    beside_all = beside_all + jnp.roll(interior, -1, axis=-3) + jnp.roll(interior, 1, axis=-3)
    return beside_all - 6.0 * interior

def base_terms(padded_base):
    centre = padded_base[..., 1:-1, 1:-1]
    gradients = jnp.stack([central_x(padded_base), central_y(padded_base), central_z(centre)])
    return (centre, gradients)

def adjoint_step(padded, centre, gradients):
    interior = padded[..., 1:-1, 1:-1]
    advect = centre[0] * central_x(padded) + centre[1] * central_y(padded) + centre[2] * central_z(interior)
    produce = lax.optimization_barrier(jnp.sum(interior[:, None] * gradients[None], axis=2))
    return interior + step_size * (advect - produce + viscosity * laplace(padded))

def project(left, right):
    return lax.dot_general(left.astype(jnp.float32), right.astype(jnp.float32), (((1,), (1,)), ((), ())), precision=lax.Precision.HIGHEST, preferred_element_type=jnp.float32)

def combine_modes(coefficients, modes):
    return jnp.dot(coefficients.T.astype(jnp.float32), modes.astype(jnp.float32), precision=lax.Precision.HIGHEST, preferred_element_type=jnp.float32)

def pad_plane(field):
    return jnp.pad(field, [(0, 0)] * (field.ndim - 2) + [(1, 1), (1, 1)])

def reference(adjoint_block, base_flow, direct_modes, dual_modes):
    row_count = 3 * NZ * NX * NY
    direct_flat = direct_modes.reshape(MODES, row_count)
    dual_flat = dual_modes.reshape(MODES, row_count)
    current = adjoint_block
    for substep in range(2):
        centre, gradients = base_terms(pad_plane(base_flow[substep]))
        advanced = adjoint_step(pad_plane(current), centre, gradients)
        flattened = advanced.reshape(VECS, row_count)
        coefficients = project(direct_flat, flattened)
        flattened = flattened - combine_modes(coefficients, dual_flat)
        current = flattened.reshape(advanced.shape)
    gram_matrix = project(flattened, flattened)
    cholesky_factor = jnp.linalg.cholesky(gram_matrix)
    solved = jax.scipy.linalg.solve_triangular(cholesky_factor, flattened, lower=True)
    next_block = (math.sqrt(row_count) * solved).reshape(adjoint_block.shape)
    return (next_block, cholesky_factor)
```

```python
import functools
import math

import jax
import jax.numpy as jnp
from jax import lax
from jax.experimental import pallas as pl
from jax.experimental.pallas import tpu as pltpu
from jax.sharding import PartitionSpec as P

step_size = 0.1
viscosity = 0.2
HALF = 0.5 * step_size
DIFF = step_size * viscosity
SUB = 8
LANES = 128


def lane_ids():
    return lax.broadcasted_iota(jnp.int32, (SUB, LANES), 1)


def row_ids():
    return lax.broadcasted_iota(jnp.int32, (SUB, LANES), 0)


def roll(x, shift, axis):
    shift %= x.shape[axis]
    return x if shift == 0 else pltpu.roll(x, shift, axis)


def block(ref, field, k):
    return ref[field, pl.ds(pl.multiple_of(k * SUB, SUB), SUB), :]


def put_block(ref, field, k, value):
    ref[field, pl.ds(pl.multiple_of(k * SUB, SUB), SUB), :] = value


def pairs_of(n):
    return [(i, j) for i in range(n) for j in range(i, n)]


def lane_sums(slots):
    half, lane = LANES // 2, lane_ids()
    while len(slots) > 1:
        count = len(slots) // 2
        low = (lane & half) == 0
        merged = []
        for one, two in zip(slots[:count], slots[count:]):
            if one is None and two is None:
                merged.append(None)
            elif two is None:
                merged.append(one + roll(one, -half, 1))
            elif one is None:
                merged.append(two + roll(two, half, 1))
            else:
                kept = jnp.where(low, one, two)
                moved = jnp.where(low, roll(one, -half, 1), roll(two, half, 1))
                merged.append(kept + moved)
        slots, half = merged, half // 2
    total = slots[0]
    while half >= 1:
        total = total + roll(total, half, 1)
        half //= 2
    for shift in (4, 2, 1):
        total = total + roll(total, shift, 0)
    return total


def spread(total, lane):
    return jnp.broadcast_to(total[:, lane : lane + 1], (SUB, LANES))


def gathered_total(ref):
    total = ref[0:SUB, :]
    for first in range(SUB, ref.shape[0], SUB):
        total = total + ref[first : first + SUB, :]
    for shift in (4, 2, 1):
        total = total + roll(total, shift, 0)
    return total


def call(kernel, outs, *args, scratch=(), vmem=None, any_args=()):
    specs = [
        pl.BlockSpec(memory_space=pl.ANY if i in any_args else pltpu.VMEM) for i in range(len(args))
    ]
    moved = sum(math.prod(a.shape) for a in args) + sum(math.prod(o) for o in outs)
    return pl.pallas_call(
        kernel,
        out_shape=[jax.ShapeDtypeStruct(shape, jnp.float32) for shape in outs],
        in_specs=specs,
        out_specs=[pl.BlockSpec(memory_space=pltpu.VMEM) for _ in outs],
        scratch_shapes=list(scratch),
        cost_estimate=pl.CostEstimate(flops=4 * moved, bytes_accessed=4 * moved, transcendentals=0),
    )(*args)


def pack_y(fields, left_ref, right_ref, blocks):
    lane = lane_ids()

    def step(k, carry):
        left = jnp.zeros((SUB, LANES), jnp.float32)
        right = left
        for n, (ref, f) in enumerate(fields):
            value = block(ref, f, k)
            left = jnp.where(lane == (2 * n - 1) % LANES, roll(value, 2 * n - 1, 1), left)
            right = jnp.where(lane == 2 * n, roll(value, 2 * n + 1, 1), right)
        rows = pl.ds(pl.multiple_of(k * SUB, SUB), SUB)
        left_ref[rows, :] = left
        right_ref[rows, :] = right
        return carry

    lax.fori_loop(0, blocks, step, 0)


def pack_x_kernel(width, groups, q_ref, base_ref, *outs):
    for (fields, first), (low, high) in zip(groups, zip(outs[::2], outs[1::2])):
        depth = low.shape[1]
        for n, (which, f) in enumerate(fields):
            ref = (q_ref, base_ref)[which]
            low[n] = ref[f, pl.ds(0, depth, stride=width), :]
            high[n] = ref[f, pl.ds(width - 1, depth, stride=width), :]


def pack_y_kernel(q_ref, base_ref, left_ref, right_ref):
    fields = [(q_ref, f) for f in range(q_ref.shape[0])]
    fields += [(base_ref, f) for f in range(base_ref.shape[0])]
    pack_y(fields, left_ref, right_ref, q_ref.shape[1] // SUB)


def modes_kernel(width, modes, slot, direct_ref, dual_ref, direct_planes, dual_planes, metric_ref):
    depth = direct_planes.shape[2]
    comps = direct_ref.shape[0] // modes
    for ref, planes in ((direct_ref, direct_planes), (dual_ref, dual_planes)):
        for f in range(ref.shape[0]):
            planes[0, f] = ref[f, pl.ds(0, depth, stride=width), :]
            planes[1, f] = ref[f, pl.ds(width - 1, depth, stride=width), :]
    todo = pairs_of(modes)
    slots = [None] * LANES
    for first in range(0, len(todo), 18):
        chunk = todo[first : first + 18]

        def step(k, accs):
            accs = list(accs)
            for c in range(comps):
                values = {m: block(dual_ref, m * comps + c, k) for m in set(sum(chunk, ()))}
                for n, (a, b) in enumerate(chunk):
                    accs[n] = accs[n] + values[a] * values[b]
            return tuple(accs)

        zero = jnp.zeros((SUB, LANES), jnp.float32)
        sums = lax.fori_loop(0, dual_ref.shape[1] // SUB, step, (zero,) * len(chunk))
        for n, value in enumerate(sums):
            slots[slot + first + n] = value
    lane = lane_ids()
    inside = (lane >= slot) & (lane < slot + len(todo))
    metric_ref[...] = jnp.where(inside, lane_sums(slots), 0.0)


def advance_kernel(width, width_comps, offset, y_offset, base_at, base_y, projections, others, *refs):
    comps = width_comps
    q_ref, base_ref, hq_l, hq_r, hb_l, hb_r = refs[:6]
    mode_refs = refs[6 : 6 + projections]
    other_refs = refs[6 + projections : 6 + projections + others]
    out_ref, planes_ref, sums_ref = refs[6 + projections + others :]
    fields, rows = out_ref.shape[:2]
    vectors, blocks = fields // comps, rows // SUB
    depth = rows // width
    lane, row = lane_ids(), row_ids()
    x_at = row % width
    low_x = jnp.where(x_at > 0, 1.0, 0.0)
    high_x = jnp.where(x_at < width - 1, 1.0, 0.0)
    upper = row < width

    def around(ref, f, k, before, after, halo, lane_at):
        here = block(ref, f, k)
        edge = roll(halo, -lane_at, 1)
        y_low = jnp.where(lane == 0, edge, roll(here, 1, 1))
        y_high = jnp.where(lane == LANES - 1, edge, roll(here, -1, 1))
        x_low, x_high = roll(here, 1, 0), roll(here, -1, 0)
        z_low, z_high = z_neighbours(here, block(ref, f, before), block(ref, f, after))
        return here, (x_low, y_low, z_low), (x_high, y_high, z_high)

    def z_neighbours(here, earlier, later):
        shift = SUB - width
        if shift == 0:
            return earlier, later
        low = roll(jnp.where(row < SUB - width, here, earlier), width, 0)
        high = roll(jnp.where(row < width, later, here), -width, 0)
        return low, high

    def step(k, carry):
        before = lax.rem(k + blocks - 1, blocks)
        after = lax.rem(k + 1, blocks)
        rows_k = pl.ds(pl.multiple_of(k * SUB, SUB), SUB)
        halo_q = hq_l[rows_k, :] + hq_r[rows_k, :]
        halo_b = hb_l[rows_k, :] + hb_r[rows_k, :]
        centre, grads = [], []
        for j in range(comps):
            here, low, high = around(base_ref, base_at + j, k, before, after, halo_b, 2 * (base_y + j))
            centre.append(HALF * here)
            grads.append(
                (
                    HALF * (high[0] * high_x - low[0] * low_x),
                    HALF * (high[1] - low[1]),
                    HALF * (high[2] - low[2]),
                )
            )
        plus = [(DIFF + centre[0]) * high_x, DIFF + centre[1], DIFF + centre[2]]
        minus = [(DIFF - centre[0]) * low_x, DIFF - centre[1], DIFF - centre[2]]
        for v in range(vectors):
            values = []
            sums = []
            for c in range(comps):
                f = v * comps + c
                here, low, high = around(
                    q_ref, offset + f, k, before, after, halo_q, 2 * (y_offset + f)
                )
                total = (1.0 - 6.0 * DIFF) * here
                for d in range(3):
                    total = total + plus[d] * high[d] + minus[d] * low[d]
                values.append(here)
                sums.append(total)
            for c in range(comps):
                total = sums[c]
                for j in range(comps):
                    total = total - values[j] * grads[j][c]
                put_block(out_ref, v * comps + c, k, total)
        return carry

    lax.fori_loop(0, blocks, step, 0)
    for f in range(fields):
        planes_ref[0, f] = out_ref[f, pl.ds(0, depth, stride=width), :]
        planes_ref[1, f] = out_ref[f, pl.ds(width - 1, depth, stride=width), :]

    zero = jnp.zeros((SUB, LANES), jnp.float32)
    at = 0
    for ref in mode_refs:
        modes = ref.shape[0] // comps

        def dots(k, accs):
            accs = list(accs)
            for c in range(comps):
                right = [block(out_ref, v * comps + c, k) for v in range(vectors)]
                for m in range(modes):
                    left = block(ref, m * comps + c, k)
                    for v in range(vectors):
                        accs[m * vectors + v] = accs[m * vectors + v] + left * right[v]
            return tuple(accs)

        for value in lax.fori_loop(0, blocks, dots, (zero,) * (modes * vectors)):
            sums_ref[at] = value
            at += 1
    if sums_ref.shape[0] > at:
        keep = (x_at > 0) & (x_at < width - 1)
        own = pairs_of(vectors)
        theirs = [(o, i, j) for o in range(others) for i in range(vectors) for j in range(vectors)]

        def gram(k, accs):
            accs = list(accs)
            for c in range(comps):
                inner = [jnp.where(keep, block(out_ref, v * comps + c, k), 0.0) for v in range(vectors)]
                for n, (i, j) in enumerate(own):
                    accs[n] = accs[n] + inner[i] * inner[j]
                for n, (o, i, j) in enumerate(theirs):
                    value = block(other_refs[o], i * comps + c, k)
                    accs[len(own) + n] = accs[len(own) + n] + value * inner[j]
            return tuple(accs)

        for value in lax.fori_loop(0, blocks, gram, (zero,) * (len(own) + len(theirs))):
            sums_ref[at] = value
            at += 1


def edge_kernel(comps, at, halo_base, lanes, others, extra, *refs):
    q_low, q_high, b_low, b_high, hq_low, hq_high, hb_low, hb_high, advanced, sums_ref = refs[:10]
    refs = refs[10:]
    modes_count = len(lanes)
    mode_refs, refs = refs[:modes_count], refs[modes_count:]
    other_refs, refs = refs[:others], refs[others:]
    extra_refs, refs = refs[:extra], refs[extra:]
    new_ref, payload_ref = refs
    q_at, base_at, hq_at, hb_at = at
    fields, depth = new_ref.shape[1:3]
    vectors, blocks = fields // comps, depth // SUB

    def delta(side, k):
        sign = (-1.0, 1.0)[side]
        own_q, own_b = (q_low, q_high)[side], (b_low, b_high)[side]
        halo_q, halo_b = (hq_low, hq_high)[side], (hb_low, hb_high)[side]
        factor = DIFF + (sign * HALF) * block(own_b, base_at, k)
        outer = [(sign * HALF) * block(halo_b, hb_at + j, k) for j in range(comps)]
        result = []
        for v in range(vectors):
            for c in range(comps):
                value = factor * block(halo_q, hq_at + v * comps + c, k)
                if c == 0:
                    for j in range(comps):
                        value = value - block(own_q, q_at + v * comps + j, k) * outer[j]
                result.append(value)
        return result

    at_sum = 0
    slots = {}
    for n, ref in enumerate(mode_refs):
        modes = ref.shape[1] // comps
        accs = tuple(sums_ref[at_sum + i] for i in range(modes * vectors))
        at_sum += modes * vectors
        for side in range(2):

            def step(k, accs, side=side, ref=ref, first=(n == 0)):
                accs = list(accs)
                changes = delta(side, k)
                for c in range(comps):
                    for m in range(modes):
                        left = ref[side, m * comps + c, pl.ds(pl.multiple_of(k * SUB, SUB), SUB), :]
                        for v in range(vectors):
                            accs[m * vectors + v] = accs[m * vectors + v] + left * changes[v * comps + c]
                if first:
                    rows = pl.ds(pl.multiple_of(k * SUB, SUB), SUB)
                    for f in range(fields):
                        new_ref[side, f, rows, :] = advanced[side, f, rows, :] + changes[f]
                return tuple(accs)

            accs = lax.fori_loop(0, blocks, step, accs)
        for i, value in enumerate(accs):
            slots[lanes[n][i]] = value
    if at_sum < sums_ref.shape[0]:
        own = pairs_of(vectors)
        theirs = [(o, i, j) for o in range(others) for i in range(vectors) for j in range(vectors)]
        accs = tuple(sums_ref[at_sum + i] for i in range(len(own) + len(theirs)))
        for side in range(2):

            def gram(k, accs, side=side):
                accs = list(accs)
                rows = pl.ds(pl.multiple_of(k * SUB, SUB), SUB)
                for c in range(comps):
                    inner = [new_ref[side, v * comps + c, rows, :] for v in range(vectors)]
                    for n, (i, j) in enumerate(own):
                        accs[n] = accs[n] + inner[i] * inner[j]
                    for n, (o, i, j) in enumerate(theirs):
                        value = other_refs[o][side, i * comps + c, rows, :]
                        accs[len(own) + n] = accs[len(own) + n] + value * inner[j]
                return tuple(accs)

            accs = lax.fori_loop(0, blocks, gram, accs)
        for i, value in enumerate(accs):
            slots[gram_lanes(lanes, i)] = value
    lane = lane_ids()
    inside = lane < 0
    for position in slots:
        inside = inside | (lane == position)
    total = jnp.where(inside, lane_sums([slots.get(i) for i in range(LANES)]), 0.0)
    for ref in extra_refs:
        total = total + ref[...]
    for first in range(0, payload_ref.shape[0], SUB):
        payload_ref[first : first + SUB, :] = total


def gram_lanes(lanes, i):
    return lanes.gram[i]


class Lanes(tuple):
    gram = ()


def deflate_planes_kernel(comps, lanes, gathered, planes, dual_planes, low_ref, high_ref, factors):
    total = gathered_total(gathered)
    for i, lane in enumerate(lanes):
        factors[i] = spread(total, lane)
    fields, depth = low_ref.shape[:2]
    vectors = fields // comps
    modes = dual_planes.shape[1] // comps
    for side, out in ((0, low_ref), (1, high_ref)):

        def step(k, carry, side=side, out=out):
            rows = pl.ds(pl.multiple_of(k * SUB, SUB), SUB)
            for c in range(comps):
                values = [planes[side, v * comps + c, rows, :] for v in range(vectors)]
                for m in range(modes):
                    mode = dual_planes[side, m * comps + c, rows, :]
                    for v in range(vectors):
                        values[v] = values[v] - factors[m * vectors + v] * mode
                for v in range(vectors):
                    out[v * comps + c, rows, :] = values[v]
            return carry

        lax.fori_loop(0, depth // SUB, step, 0)


def deflate_kernel(
    width, comps, lanes, gathered, advanced, dual, low_ref, high_ref, out_ref, left_ref, right_ref, factors
):
    total = gathered_total(gathered)
    for i, lane in enumerate(lanes):
        factors[i] = spread(total, lane)
    fields, rows_all = out_ref.shape[:2]
    vectors = fields // comps
    modes = dual.shape[0] // comps

    def step(k, carry):
        for c in range(comps):
            values = [block(advanced, v * comps + c, k) for v in range(vectors)]
            for m in range(modes):
                mode = block(dual, m * comps + c, k)
                for v in range(vectors):
                    values[v] = values[v] - factors[m * vectors + v] * mode
            for v in range(vectors):
                put_block(out_ref, v * comps + c, k, values[v])
        return carry

    lax.fori_loop(0, rows_all // SUB, step, 0)
    depth = rows_all // width
    for f in range(fields):
        out_ref[f, pl.ds(0, depth, stride=width), :] = low_ref[f]
        out_ref[f, pl.ds(width - 1, depth, stride=width), :] = high_ref[f]
    pack_y([(out_ref, f) for f in range(fields)], left_ref, right_ref, rows_all // SUB)


def finish_kernel(width, comps, layout, scale, groups, *refs):
    gathered, dual = refs[:2]
    advanced = refs[2 : 2 + groups]
    planes = refs[2 + groups : 2 + 2 * groups]
    out_ref, growth_ref, block_ref, factors, semaphore = refs[2 + 2 * groups :]
    fields, rows_all = out_ref.shape[:2]
    vectors, modes = fields // comps, dual.shape[0] // comps
    each = fields // groups
    copies = [
        pltpu.make_async_copy(advanced[g], block_ref.at[pl.ds(g * each, each)], semaphore.at[g])
        for g in range(groups)
    ]
    for copy in copies:
        copy.start()
    total = gathered_total(gathered)
    first, cross, self_gram, metric = layout
    coef = {key: spread(total, lane) for key, lane in first.items()}
    mixed = {key: spread(total, lane) for key, lane in cross.items()}
    inner = {key: spread(total, lane) for key, lane in self_gram.items()}
    weight = {key: spread(total, lane) for key, lane in metric.items()}
    weighted = {}
    for m in range(modes):
        for j in range(vectors):
            weighted[m, j] = sum(weight[min(m, n), max(m, n)] * coef[n, j] for n in range(modes))
    gram = {}
    for i, j in pairs_of(vectors):
        value = inner[i, j]
        for m in range(modes):
            value = value - coef[m, i] * (mixed[m, j] - weighted[m, j]) - coef[m, j] * mixed[m, i]
        gram[j, i] = value
    lower, inverse_diagonal = {}, {}
    for j in range(vectors):
        value = gram[j, j]
        for n in range(j):
            value = value - lower[j, n] * lower[j, n]
        lower[j, j] = jnp.sqrt(value)
        inverse_diagonal[j] = 1.0 / lower[j, j]
        for i in range(j + 1, vectors):
            value = gram[i, j]
            for n in range(j):
                value = value - lower[i, n] * lower[j, n]
            lower[i, j] = value * inverse_diagonal[j]
    inverse = {}
    for j in range(vectors):
        inverse[j, j] = inverse_diagonal[j]
        for i in range(j + 1, vectors):
            value = sum(lower[i, n] * inverse[n, j] for n in range(j, i))
            inverse[i, j] = -inverse_diagonal[i] * value
    row, lane = row_ids(), lane_ids()
    growth = jnp.zeros((SUB, LANES), jnp.float32)
    for (i, j), value in lower.items():
        growth = jnp.where((row == i) & (lane == j), value, growth)
    growth_ref[...] = growth[:vectors, :vectors]
    at = {}
    for (i, j), value in inverse.items():
        at[i, j] = len(at)
        factors[at[i, j]] = scale * value
    mode_at = {}
    for i in range(vectors):
        for m in range(modes):
            mode_at[i, m] = len(at) + len(mode_at)
            factors[mode_at[i, m]] = -scale * sum(inverse[i, j] * coef[m, j] for j in range(i + 1))
    for copy in copies:
        copy.wait()
    depth = rows_all // width
    for g in range(groups):
        for f in range(each):
            block_ref[g * each + f, pl.ds(0, depth, stride=width), :] = planes[g][0, f]
            block_ref[g * each + f, pl.ds(width - 1, depth, stride=width), :] = planes[g][1, f]

    def step(k, carry):
        for c in range(comps):
            parts = [block(block_ref, v * comps + c, k) for v in range(vectors)]
            values = []
            for i in range(vectors):
                value = factors[at[i, 0]] * parts[0]
                for j in range(1, i + 1):
                    value = value + factors[at[i, j]] * parts[j]
                values.append(value)
            for m in range(modes):
                mode = block(dual, m * comps + c, k)
                for i in range(vectors):
                    values[i] = values[i] + factors[mode_at[i, m]] * mode
            for i in range(vectors):
                put_block(out_ref, i * comps + c, k, values[i])
        return carry

    lax.fori_loop(0, rows_all // SUB, step, 0)


def shift(field, axis, up):
    count = lax.axis_size(axis)
    pairs = [(i, i + 1) for i in range(count - 1)]
    return lax.ppermute(field, axis, pairs if up else [(j, i) for i, j in pairs])


def halos(low, high, axis):
    return shift(high, axis, True), shift(low, axis, False)


def exchange(payload):
    return lax.all_to_all(payload, ("gx", "gy"), 0, 0, tiled=True)


def body(adjoint_block, base_flow, direct_modes, dual_modes):
    vectors, comps, depth, width, length = adjoint_block.shape
    steps, modes = base_flow.shape[0], direct_modes.shape[0]
    rows = depth * width
    assert length == LANES and SUB % width == 0 and rows % SUB == 0 and depth % SUB == 0
    devices = lax.axis_size("gx") * lax.axis_size("gy")
    cells = float(comps * rows * length * devices)
    groups = 2
    size = vectors // groups
    part = size * comps

    q = adjoint_block.reshape(vectors * comps, rows, length)
    base = base_flow.reshape(steps * comps, rows, length)
    direct = direct_modes.reshape(modes * comps, rows, length)
    dual = dual_modes.reshape(modes * comps, rows, length)

    plane = (depth, length)
    sets = []
    for g in range(groups):
        fields = [(0, g * part + f) for f in range(part)]
        if g == 0:
            fields += [(1, j) for j in range(comps)]
        sets.append((fields, None))
    sets.append(([(1, comps + j) for j in range(comps)], None))
    packed = call(
        functools.partial(pack_x_kernel, width, sets),
        [(len(fields), *plane) for fields, _ in sets for _ in range(2)],
        q,
        base,
    )
    lows, highs = packed[::2], packed[1::2]
    halo_x = [halos(low, high, "gx") for low, high in zip(lows, highs)]
    left, right = call(pack_y_kernel, [(rows, LANES)] * 2, q, base)
    halo_y = halos(left, right, "gy")

    pairs, mode_pairs = pairs_of(vectors), pairs_of(modes)
    first = {(m, i): m * vectors + i for m in range(modes) for i in range(vectors)}
    cross = {key: modes * vectors + lane for key, lane in first.items()}
    self_gram = {key: 2 * modes * vectors + n for n, key in enumerate(pairs)}
    slot = 2 * modes * vectors + len(pairs)
    metric = {key: slot + n for n, key in enumerate(mode_pairs)}
    assert slot + len(mode_pairs) <= LANES
    direct_planes, dual_planes, metric_part = call(
        functools.partial(modes_kernel, width, modes, slot),
        [(2, modes * comps, *plane)] * 2 + [(SUB, LANES)],
        direct,
        dual,
    )

    spacing = LANES // (1 << (modes * size - 1).bit_length())
    group_lanes = [spacing * n for n in range(modes * size)]
    advanced, gathered, edge = [], [], []
    for g in range(groups):
        kernel = functools.partial(advance_kernel, width, comps, g * part, g * part, 0, vectors * comps, 1, 0)
        out, planes, sums = call(
            kernel,
            [(part, rows, length), (2, part, *plane), (modes * size, SUB, LANES)],
            q,
            base,
            *halo_y,
            *halo_y,
            direct,
        )
        lanes = Lanes([group_lanes])
        new, payload = call(
            functools.partial(edge_kernel, comps, (0, part, 0, part), None, lanes, 0, 0),
            [(2, part, *plane), (devices, LANES)],
            lows[g],
            highs[g],
            lows[0],
            highs[0],
            *halo_x[g],
            *halo_x[0],
            planes,
            sums,
            direct_planes,
        )
        advanced.append(out)
        edge.append(new)
        gathered.append(exchange(payload))

    blocks, planes_new, parts = [], [], [metric_part]
    for g in range(groups):
        scratch = [pltpu.VMEM((modes * size, SUB, LANES), jnp.float32)]
        low, high = call(
            functools.partial(deflate_planes_kernel, comps, group_lanes),
            [(part, *plane)] * 2,
            gathered[g],
            edge[g],
            dual_planes,
            scratch=scratch,
        )
        outer_x = halos(low, high, "gx")
        current, left, right = call(
            functools.partial(deflate_kernel, width, comps, group_lanes),
            [(part, rows, length), (rows, LANES), (rows, LANES)],
            gathered[g],
            advanced[g],
            dual,
            low,
            high,
            scratch=scratch,
        )
        outer_y = halos(left, right, "gy")
        kernel = functools.partial(
            advance_kernel, width, comps, 0, 0, comps, vectors * comps + comps, 2, len(blocks)
        )
        grams = size * (size + 1) // 2 + len(blocks) * size * size
        out, planes, sums = call(
            kernel,
            [(part, rows, length), (2, part, *plane), (2 * modes * size + grams, SUB, LANES)],
            current,
            base,
            *outer_y,
            *halo_y,
            direct,
            dual,
            *blocks,
        )
        own = [g * size + i for i in range(size)]
        lanes = Lanes(
            [[table[m, i] for m in range(modes) for i in own] for table in (first, cross)]
        )
        lanes.gram = [self_gram[own[i], own[j]] for i, j in pairs_of(size)]
        lanes.gram += [self_gram[o * size + i, j] for o in range(len(blocks)) for i in range(size) for j in own]
        new, payload = call(
            functools.partial(
                edge_kernel, comps, (0, 0, 0, 0), None, lanes, len(blocks), len(parts) if g == groups - 1 else 0
            ),
            [(2, part, *plane), (devices if g == groups - 1 else SUB, LANES)],
            low,
            high,
            lows[groups],
            highs[groups],
            *outer_x,
            *halo_x[groups],
            planes,
            sums,
            direct_planes,
            dual_planes,
            *planes_new,
            *(parts if g == groups - 1 else ()),
        )
        blocks.append(out)
        planes_new.append(new)
        parts.append(payload)

    total = exchange(parts[-1])
    factor_count = vectors * (vectors + 1) // 2 + modes * vectors
    next_block, growth = call(
        functools.partial(
            finish_kernel, width, comps, (first, cross, self_gram, metric), math.sqrt(cells), groups
        ),
        [(vectors * comps, rows, length), (vectors, vectors)],
        total,
        dual,
        *blocks,
        *planes_new,
        scratch=[
            pltpu.VMEM((vectors * comps, rows, length), jnp.float32),
            pltpu.VMEM((factor_count, SUB, LANES), jnp.float32),
            pltpu.SemaphoreType.DMA((groups,)),
        ],
        any_args=tuple(range(2, 2 + groups)),
    )
    return (next_block.reshape(adjoint_block.shape), growth)


def solution(mesh):
    placed = P(None, None, None, "gx", "gy")
    return jax.shard_map(
        body,
        mesh=mesh,
        in_specs=(placed,) * 4,
        out_specs=(placed, P()),
        check_vma=False,
    )
```

```python
import functools
import math

import jax
import jax.numpy as jnp
from jax import lax
from jax.experimental import pallas as pl
from jax.experimental.pallas import tpu as pltpu
from jax.sharding import PartitionSpec as P

step_size = 0.1
viscosity = 0.2
HALF = 0.5 * step_size
DIFF = step_size * viscosity
SUB = 8
LANES = 128


def lane_ids():
    return lax.broadcasted_iota(jnp.int32, (SUB, LANES), 1)


def row_ids():
    return lax.broadcasted_iota(jnp.int32, (SUB, LANES), 0)


def roll(x, shift, axis):
    shift %= x.shape[axis]
    return x if shift == 0 else pltpu.roll(x, shift, axis)


def block(ref, field, k):
    return ref[field, pl.ds(pl.multiple_of(k * SUB, SUB), SUB), :]


def put_block(ref, field, k, value):
    ref[field, pl.ds(pl.multiple_of(k * SUB, SUB), SUB), :] = value


def pairs_of(n):
    return [(i, j) for i in range(n) for j in range(i, n)]


def lane_sums(slots):
    half, lane = LANES // 2, lane_ids()
    while len(slots) > 1:
        count = len(slots) // 2
        low = (lane & half) == 0
        merged = []
        for one, two in zip(slots[:count], slots[count:]):
            if one is None and two is None:
                merged.append(None)
            elif two is None:
                merged.append(one + roll(one, -half, 1))
            elif one is None:
                merged.append(two + roll(two, half, 1))
            else:
                kept = jnp.where(low, one, two)
                moved = jnp.where(low, roll(one, -half, 1), roll(two, half, 1))
                merged.append(kept + moved)
        slots, half = merged, half // 2
    total = slots[0]
    while half >= 1:
        total = total + roll(total, half, 1)
        half //= 2
    for shift in (4, 2, 1):
        total = total + roll(total, shift, 0)
    return total


def spread(total, lane):
    return jnp.broadcast_to(total[:, lane : lane + 1], (SUB, LANES))


def gathered_total(ref):
    total = ref[0:SUB, :]
    for first in range(SUB, ref.shape[0], SUB):
        total = total + ref[first : first + SUB, :]
    for shift in (4, 2, 1):
        total = total + roll(total, shift, 0)
    return total


def call(kernel, micros, outs, *args, scratch=(), any_args=()):
    specs = [
        pl.BlockSpec(memory_space=pl.ANY if i in any_args else pltpu.VMEM) for i in range(len(args))
    ]
    shapes = [a.shape for i, a in enumerate(args) if i not in any_args] + list(outs)
    shapes += [ref.shape for ref in scratch if ref is not pltpu.SemaphoreType.DMA]
    held = sum(4 * math.prod((*shape[:-1], LANES)) for shape in shapes)
    return pl.pallas_call(
        kernel,
        out_shape=[jax.ShapeDtypeStruct(shape, jnp.float32) for shape in outs],
        in_specs=specs,
        out_specs=[pl.BlockSpec(memory_space=pltpu.VMEM) for _ in outs],
        scratch_shapes=list(scratch),
        compiler_params=pltpu.CompilerParams(vmem_limit_bytes=held + (2 << 20)),
        cost_estimate=pl.CostEstimate(
            flops=0, bytes_accessed=int(micros * 3.5e6), transcendentals=0
        ),
    )(*args)


def sides(width):
    even = lax.rem(lax.axis_index("gx"), 2) == 0
    first = jnp.where(even, width - 1, 0)
    sign = jnp.where(even, 1.0, -1.0)
    return (first, width - 1 - first), (sign, -sign)


def pack_y(fields, first_ref, second_ref, blocks):
    lane = lane_ids()
    even = lax.rem(lax.axis_index("gy"), 2) == 0

    def step(k, carry):
        left = jnp.zeros((SUB, LANES), jnp.float32)
        right = left
        for n, (ref, f) in enumerate(fields):
            value = block(ref, f, k)
            left = jnp.where(lane == (2 * n - 1) % LANES, roll(value, 2 * n - 1, 1), left)
            right = jnp.where(lane == 2 * n, roll(value, 2 * n + 1, 1), right)
        rows = pl.ds(pl.multiple_of(k * SUB, SUB), SUB)
        first_ref[rows, :] = jnp.where(even, right, left)
        second_ref[rows, :] = jnp.where(even, left, right)
        return carry

    lax.fori_loop(0, blocks, step, 0, unroll=4)


def pack_x_kernel(width, sets, q_ref, base_ref, *outs):
    layers, _ = sides(width)
    for fields, pair in zip(sets, zip(outs[::2], outs[1::2])):
        for out, x in zip(pair, layers):
            for n, (which, f) in enumerate(fields):
                ref = (q_ref, base_ref)[which]
                out[n] = ref[f, pl.ds(x, out.shape[1], stride=width), :]


def pack_y_kernel(q_ref, base_ref, first_ref, second_ref):
    fields = [(q_ref, f) for f in range(q_ref.shape[0])]
    fields += [(base_ref, f) for f in range(base_ref.shape[0])]
    pack_y(fields, first_ref, second_ref, q_ref.shape[1] // SUB)


def modes_kernel(width, modes, slot, direct_ref, dual_ref, direct_planes, dual_planes, metric_ref):
    depth = direct_planes.shape[2]
    comps = direct_ref.shape[0] // modes
    layers, _ = sides(width)
    for ref, planes in ((direct_ref, direct_planes), (dual_ref, dual_planes)):
        for f in range(ref.shape[0]):
            for side, x in enumerate(layers):
                planes[side, f] = ref[f, pl.ds(x, depth, stride=width), :]
    todo = pairs_of(modes)
    slots = [None] * LANES

    def step(k, accs):
        accs = list(accs)
        for c in range(comps):
            values = [block(dual_ref, m * comps + c, k) for m in range(modes)]
            for n, (a, b) in enumerate(todo):
                accs[n] = accs[n] + values[a] * values[b]
        return tuple(accs)

    zero = jnp.zeros((SUB, LANES), jnp.float32)
    sums = lax.fori_loop(0, dual_ref.shape[1] // SUB, step, (zero,) * len(todo))
    for n, value in enumerate(sums):
        slots[slot + n] = value
    lane = lane_ids()
    inside = (lane >= slot) & (lane < slot + len(todo))
    metric_ref[...] = jnp.where(inside, lane_sums(slots), 0.0)


def advance_kernel(width, comps, base_at, base_y, projections, *refs):
    q_ref, base_ref, hq_l, hq_r, hb_l, hb_r = refs[:6]
    mode_refs = refs[6 : 6 + projections]
    out_ref, planes_ref, sums_ref = refs[6 + projections :]
    fields, rows = out_ref.shape[:2]
    vectors, blocks = fields // comps, rows // SUB
    depth = rows // width
    lane, row = lane_ids(), row_ids()
    x_at = row % width
    low_x = jnp.where(x_at > 0, 1.0, 0.0)
    high_x = jnp.where(x_at < width - 1, 1.0, 0.0)
    upper = row < width

    def around(ref, f, k, before, after, halo, lane_at):
        here = block(ref, f, k)
        edge = roll(halo, -lane_at, 1)
        y_low = jnp.where(lane == 0, edge, roll(here, 1, 1))
        y_high = jnp.where(lane == LANES - 1, edge, roll(here, -1, 1))
        x_low, x_high = roll(here, 1, 0), roll(here, -1, 0)
        z_low, z_high = z_neighbours(here, block(ref, f, before), block(ref, f, after))
        return here, (x_low, y_low, z_low), (x_high, y_high, z_high)

    def z_neighbours(here, earlier, later):
        shift = SUB - width
        if shift == 0:
            return earlier, later
        low = roll(jnp.where(row < SUB - width, here, earlier), width, 0)
        high = roll(jnp.where(row < width, later, here), -width, 0)
        return low, high

    def step(k, carry):
        before = lax.rem(k + blocks - 1, blocks)
        after = lax.rem(k + 1, blocks)
        rows_k = pl.ds(pl.multiple_of(k * SUB, SUB), SUB)
        halo_q = hq_l[rows_k, :] + hq_r[rows_k, :]
        halo_b = hb_l[rows_k, :] + hb_r[rows_k, :]
        centre, grads = [], []
        for j in range(comps):
            here, low, high = around(base_ref, base_at + j, k, before, after, halo_b, 2 * (base_y + j))
            centre.append(HALF * here)
            grads.append(
                (
                    HALF * (high[0] * high_x - low[0] * low_x),
                    HALF * (high[1] - low[1]),
                    HALF * (high[2] - low[2]),
                )
            )
        plus = [(DIFF + centre[0]) * high_x, DIFF + centre[1], DIFF + centre[2]]
        minus = [(DIFF - centre[0]) * low_x, DIFF - centre[1], DIFF - centre[2]]
        for v in range(vectors):
            values = []
            sums = []
            for c in range(comps):
                f = v * comps + c
                here, low, high = around(
                    q_ref, f, k, before, after, halo_q, 2 * f
                )
                total = (1.0 - 6.0 * DIFF) * here
                for d in range(3):
                    total = total + plus[d] * high[d] + minus[d] * low[d]
                values.append(here)
                sums.append(total)
            for c in range(comps):
                total = sums[c]
                for j in range(comps):
                    total = total - values[j] * grads[j][c]
                put_block(out_ref, v * comps + c, k, total)
        return carry

    lax.fori_loop(0, blocks, step, 0)
    layers, _ = sides(width)
    for f in range(fields):
        for side, x in enumerate(layers):
            planes_ref[side, f] = out_ref[f, pl.ds(x, depth, stride=width), :]

    zero = jnp.zeros((SUB, LANES), jnp.float32)
    at = 0
    for ref in mode_refs:
        modes = ref.shape[0] // comps

        def dots(k, accs):
            accs = list(accs)
            for c in range(comps):
                right = [block(out_ref, v * comps + c, k) for v in range(vectors)]
                for m in range(modes):
                    left = block(ref, m * comps + c, k)
                    for v in range(vectors):
                        accs[m * vectors + v] = accs[m * vectors + v] + left * right[v]
            return tuple(accs)

        for value in lax.fori_loop(0, blocks, dots, (zero,) * (modes * vectors)):
            sums_ref[at] = value
            at += 1
    if sums_ref.shape[0] > at:
        keep = (x_at > 0) & (x_at < width - 1)
        own = pairs_of(vectors)

        def gram(k, accs):
            accs = list(accs)
            for c in range(comps):
                inner = [jnp.where(keep, block(out_ref, v * comps + c, k), 0.0) for v in range(vectors)]
                for n, (i, j) in enumerate(own):
                    accs[n] = accs[n] + inner[i] * inner[j]
            return tuple(accs)

        for value in lax.fori_loop(0, blocks, gram, (zero,) * len(own)):
            sums_ref[at] = value
            at += 1


def edge_kernel(width, comps, at, lanes, projections, extra, *refs):
    own_q, own_b, halo_q, halo_b = (refs[n : n + 2] for n in (0, 2, 4, 6))
    advanced, sums_ref = refs[8:10]
    mode_refs, refs = refs[10 : 10 + projections], refs[10 + projections :]
    extra_refs, (new_ref, payload_ref) = refs[:extra], refs[extra:]
    fields, depth = new_ref.shape[1:3]
    vectors, blocks = fields // comps, depth // SUB
    _, signs = sides(width)

    def step(k, carry):
        rows = pl.ds(pl.multiple_of(k * SUB, SUB), SUB)
        for side in range(2):
            scale = signs[side] * HALF
            factor = DIFF + scale * own_b[side][at[0], rows, :]
            outer = [scale * halo_b[side][at[1] + j, rows, :] for j in range(comps)]
            for v in range(vectors):
                for c in range(comps):
                    value = factor * halo_q[side][v * comps + c, rows, :]
                    if c == 0:
                        for j in range(comps):
                            value = value - own_q[side][v * comps + j, rows, :] * outer[j]
                    new_ref[side, v * comps + c, rows, :] = value
        return carry

    lax.fori_loop(0, blocks, step, 0)
    at_sum = 0
    slots = {}
    for n, ref in enumerate(mode_refs):
        modes = ref.shape[1] // comps
        accs = tuple(sums_ref[at_sum + i] for i in range(modes * vectors))
        at_sum += modes * vectors

        def dots(k, accs, ref=ref):
            accs = list(accs)
            rows = pl.ds(pl.multiple_of(k * SUB, SUB), SUB)
            for side in range(2):
                for c in range(comps):
                    right = [new_ref[side, v * comps + c, rows, :] for v in range(vectors)]
                    for m in range(modes):
                        left = ref[side, m * comps + c, rows, :]
                        for v in range(vectors):
                            accs[m * vectors + v] = accs[m * vectors + v] + left * right[v]
            return tuple(accs)

        for lane, value in zip(lanes[n], lax.fori_loop(0, blocks, dots, accs)):
            slots[lane] = value
    own = pairs_of(vectors)
    squares = at_sum < sums_ref.shape[0]
    accs = tuple(sums_ref[at_sum + i] for i in range(len(own))) if squares else ()

    def finish(k, accs):
        accs = list(accs)
        rows = pl.ds(pl.multiple_of(k * SUB, SUB), SUB)
        for side in range(2):
            for c in range(comps):
                inner = []
                for v in range(vectors):
                    f = v * comps + c
                    inner.append(new_ref[side, f, rows, :] + advanced[side, f, rows, :])
                    new_ref[side, f, rows, :] = inner[v]
                if squares:
                    for n, (i, j) in enumerate(own):
                        accs[n] = accs[n] + inner[i] * inner[j]
        return tuple(accs)

    for lane, value in zip(lanes[-1] if squares else (), lax.fori_loop(0, blocks, finish, accs)):
        slots[lane] = value
    lane = lane_ids()
    inside = lane < 0
    for position in slots:
        inside = inside | (lane == position)
    total = jnp.where(inside, lane_sums([slots.get(i) for i in range(LANES)]), 0.0)
    for ref in extra_refs:
        total = total + ref[...]
    for first in range(0, payload_ref.shape[0], SUB):
        payload_ref[first : first + SUB, :] = total


def deflate_planes_kernel(comps, lanes, gathered, planes, dual_planes, first_ref, second_ref, factors):
    total = gathered_total(gathered)
    for i, lane in enumerate(lanes):
        factors[i] = spread(total, lane)
    fields, depth = first_ref.shape[:2]
    vectors = fields // comps
    modes = dual_planes.shape[1] // comps
    for side, out in ((0, first_ref), (1, second_ref)):

        def step(k, carry, side=side, out=out):
            rows = pl.ds(pl.multiple_of(k * SUB, SUB), SUB)
            for c in range(comps):
                values = [planes[side, v * comps + c, rows, :] for v in range(vectors)]
                for m in range(modes):
                    mode = dual_planes[side, m * comps + c, rows, :]
                    for v in range(vectors):
                        values[v] = values[v] - factors[m * vectors + v] * mode
                for v in range(vectors):
                    out[v * comps + c, rows, :] = values[v]
            return carry

        lax.fori_loop(0, depth // SUB, step, 0)


def deflate_kernel(
    width, comps, lanes, gathered, advanced, dual, planes_a, planes_b, out_ref, first_ref, second_ref, factors
):
    total = gathered_total(gathered)
    for i, lane in enumerate(lanes):
        factors[i] = spread(total, lane)
    fields, rows_all = out_ref.shape[:2]
    vectors = fields // comps
    modes = dual.shape[0] // comps

    def step(k, carry):
        for c in range(comps):
            values = [block(advanced, v * comps + c, k) for v in range(vectors)]
            for m in range(modes):
                mode = block(dual, m * comps + c, k)
                for v in range(vectors):
                    values[v] = values[v] - factors[m * vectors + v] * mode
            for v in range(vectors):
                put_block(out_ref, v * comps + c, k, values[v])
        return carry

    lax.fori_loop(0, rows_all // SUB, step, 0)
    depth = rows_all // width
    layers, _ = sides(width)
    for f in range(fields):
        for planes, x in zip((planes_a, planes_b), layers):
            out_ref[f, pl.ds(x, depth, stride=width), :] = planes[f]
    pack_y([(out_ref, f) for f in range(fields)], first_ref, second_ref, rows_all // SUB)


def finish_kernel(width, comps, layout, scale, *refs):
    gathered, dual, advanced, planes, out_ref, growth_ref, block_ref, factors, semaphore = refs
    fields, rows_all = out_ref.shape[:2]
    vectors, modes = fields // comps, dual.shape[0] // comps
    copy = pltpu.make_async_copy(advanced, block_ref, semaphore)
    copy.start()
    total = gathered_total(gathered)
    first, cross, self_gram, metric = layout
    coef = {key: spread(total, lane) for key, lane in first.items()}
    mixed = {key: spread(total, lane) for key, lane in cross.items()}
    inner = {key: spread(total, lane) for key, lane in self_gram.items()}
    weight = {key: spread(total, lane) for key, lane in metric.items()}
    weighted = {}
    for m in range(modes):
        for j in range(vectors):
            weighted[m, j] = sum(weight[min(m, n), max(m, n)] * coef[n, j] for n in range(modes))
    gram = {}
    for i, j in pairs_of(vectors):
        value = inner[i, j]
        for m in range(modes):
            value = value - coef[m, i] * (mixed[m, j] - weighted[m, j]) - coef[m, j] * mixed[m, i]
        gram[j, i] = value
    lower, inverse_diagonal = {}, {}
    for j in range(vectors):
        value = gram[j, j]
        for n in range(j):
            value = value - lower[j, n] * lower[j, n]
        lower[j, j] = jnp.sqrt(value)
        inverse_diagonal[j] = 1.0 / lower[j, j]
        for i in range(j + 1, vectors):
            value = gram[i, j]
            for n in range(j):
                value = value - lower[i, n] * lower[j, n]
            lower[i, j] = value * inverse_diagonal[j]
    inverse = {}
    for j in range(vectors):
        inverse[j, j] = inverse_diagonal[j]
        for i in range(j + 1, vectors):
            value = sum(lower[i, n] * inverse[n, j] for n in range(j, i))
            inverse[i, j] = -inverse_diagonal[i] * value
    row, lane = row_ids(), lane_ids()
    growth = jnp.zeros((SUB, LANES), jnp.float32)
    for (i, j), value in lower.items():
        growth = jnp.where((row == i) & (lane == j), value, growth)
    growth_ref[...] = growth[:vectors, :vectors]
    at = {}
    for (i, j), value in inverse.items():
        at[i, j] = len(at)
        factors[at[i, j]] = scale * value
    mode_at = {}
    for i in range(vectors):
        for m in range(modes):
            mode_at[i, m] = len(at) + len(mode_at)
            factors[mode_at[i, m]] = -scale * sum(inverse[i, j] * coef[m, j] for j in range(i + 1))
    copy.wait()
    depth = rows_all // width
    layers, _ = sides(width)
    for f in range(fields):
        for side, x in enumerate(layers):
            block_ref[f, pl.ds(x, depth, stride=width), :] = planes[side, f]

    def step(k, carry):
        for c in range(comps):
            parts = [block(block_ref, v * comps + c, k) for v in range(vectors)]
            values = []
            for i in range(vectors):
                value = factors[at[i, 0]] * parts[0]
                for j in range(1, i + 1):
                    value = value + factors[at[i, j]] * parts[j]
                values.append(value)
            for m in range(modes):
                mode = block(dual, m * comps + c, k)
                for i in range(vectors):
                    values[i] = values[i] + factors[mode_at[i, m]] * mode
            for i in range(vectors):
                put_block(out_ref, i * comps + c, k, values[i])
        return carry

    lax.fori_loop(0, rows_all // SUB, step, 0)


def swap(first, second, axis):
    count = lax.axis_size(axis)
    results = []
    for field, start in ((first, 0), (second, 1)):
        pairs = [(i, i + 1) for i in range(start, count - 1, 2)]
        results.append(lax.ppermute(field, axis, pairs + [(j, i) for i, j in pairs]))
    return results


def exchange(payload):
    return lax.all_to_all(payload, ("gx", "gy"), 0, 0, tiled=True)


def body(adjoint_block, base_flow, direct_modes, dual_modes):
    vectors, comps, depth, width, length = adjoint_block.shape
    steps, modes = base_flow.shape[0], direct_modes.shape[0]
    rows = depth * width
    assert length == LANES and SUB % width == 0 and rows % SUB == 0 and depth % SUB == 0
    devices = lax.axis_size("gx") * lax.axis_size("gy")
    cells = float(comps * rows * length * devices)
    fields = vectors * comps

    q = adjoint_block.reshape(fields, rows, length)
    base = base_flow.reshape(steps * comps, rows, length)
    direct = direct_modes.reshape(modes * comps, rows, length)
    dual = dual_modes.reshape(modes * comps, rows, length)
    plane = (depth, length)

    sets = [
        [(0, f) for f in range(fields)] + [(1, j) for j in range(comps)],
        [(1, comps + j) for j in range(comps)],
    ]
    *layers, late_a, late_b = call(
        functools.partial(pack_x_kernel, width, sets),
        2.5,
        [(len(some), *plane) for some in sets for _ in range(2)],
        q,
        base,
    )
    halo_x = swap(*layers, "gx")
    halo_y = swap(*call(pack_y_kernel, 3, [(rows, LANES)] * 2, q, base), "gy")

    pairs, mode_pairs = pairs_of(vectors), pairs_of(modes)
    first = {(m, i): m * vectors + i for m in range(modes) for i in range(vectors)}
    cross = {key: modes * vectors + lane for key, lane in first.items()}
    self_gram = {key: 2 * modes * vectors + n for n, key in enumerate(pairs)}
    slot = 2 * modes * vectors + len(pairs)
    metric = {key: slot + n for n, key in enumerate(mode_pairs)}
    assert slot + len(mode_pairs) <= LANES
    direct_planes, dual_planes, metric_part = call(
        functools.partial(modes_kernel, width, modes, slot),
        4,
        [(2, modes * comps, *plane)] * 2 + [(SUB, LANES)],
        direct,
        dual,
    )

    spacing = LANES // (1 << (modes * vectors - 1).bit_length())
    spaced = [spacing * n for n in range(modes * vectors)]
    advanced, planes, sums = call(
        functools.partial(advance_kernel, width, comps, 0, fields, 1),
        8,
        [(fields, rows, length), (2, fields, *plane), (modes * vectors, SUB, LANES)],
        q,
        base,
        *halo_y,
        *halo_y,
        direct,
    )
    edge, payload = call(
        functools.partial(edge_kernel, width, comps, (fields, fields), [spaced], 1, 0),
        2,
        [(2, fields, *plane), (devices, LANES)],
        *layers,
        *layers,
        *halo_x,
        *halo_x,
        planes,
        sums,
        direct_planes,
    )
    payload, late_a, late_b = lax.optimization_barrier((payload, late_a, late_b))
    halo_late = swap(late_a, late_b, "gx")
    gathered = exchange(payload)

    scratch = [pltpu.VMEM((modes * vectors, SUB, LANES), jnp.float32)]
    layers = call(
        functools.partial(deflate_planes_kernel, comps, spaced),
        1.5,
        [(fields, *plane)] * 2,
        gathered,
        edge,
        dual_planes,
        scratch=scratch,
    )
    halo_x = swap(*layers, "gx")
    current, *columns = call(
        functools.partial(deflate_kernel, width, comps, spaced),
        3,
        [(fields, rows, length), (rows, LANES), (rows, LANES)],
        gathered,
        advanced,
        dual,
        *layers,
        scratch=scratch,
    )
    columns = swap(*columns, "gy")
    advanced, planes, sums = call(
        functools.partial(advance_kernel, width, comps, comps, fields + comps, 2),
        12,
        [(fields, rows, length), (2, fields, *plane), (2 * modes * vectors + len(pairs), SUB, LANES)],
        current,
        base,
        *columns,
        *halo_y,
        direct,
        dual,
    )
    lanes = [list(first.values()), list(cross.values()), list(self_gram.values())]
    edge, payload = call(
        functools.partial(edge_kernel, width, comps, (0, 0), lanes, 2, 1),
        3,
        [(2, fields, *plane), (devices, LANES)],
        *layers,
        late_a,
        late_b,
        *halo_x,
        *halo_late,
        planes,
        sums,
        direct_planes,
        dual_planes,
        metric_part,
    )
    total = exchange(payload)
    factor_count = vectors * (vectors + 1) // 2 + modes * vectors
    next_block, growth = call(
        functools.partial(finish_kernel, width, comps, (first, cross, self_gram, metric), math.sqrt(cells)),
        5,
        [(fields, rows, length), (vectors, vectors)],
        total,
        dual,
        advanced,
        edge,
        scratch=[
            pltpu.VMEM((fields, rows, length), jnp.float32),
            pltpu.VMEM((factor_count, SUB, LANES), jnp.float32),
            pltpu.SemaphoreType.DMA,
        ],
        any_args=(2,),
    )
    return (next_block.reshape(adjoint_block.shape), growth)


def solution(mesh):
    placed = P(None, None, None, "gx", "gy")
    return jax.shard_map(
        body,
        mesh=mesh,
        in_specs=(placed,) * 4,
        out_specs=(placed, P()),
        check_vma=False,
    )
```

```python
import functools
import math

import jax
import jax.numpy as jnp
from jax import lax
from jax.experimental import pallas as pl
from jax.experimental.pallas import tpu as pltpu
from jax.sharding import PartitionSpec as P


step_size = 0.1
viscosity = 0.2
HALF = 0.5 * step_size
DIFF = step_size * viscosity
SUB = 8
LANES = 128


def lane_ids():
    return lax.broadcasted_iota(jnp.int32, (SUB, LANES), 1)


def row_ids():
    return lax.broadcasted_iota(jnp.int32, (SUB, LANES), 0)


def roll(x, shift, axis):
    shift %= x.shape[axis]
    return x if shift == 0 else pltpu.roll(x, shift, axis)


def block(ref, field, k):
    return ref[field, pl.ds(pl.multiple_of(k * SUB, SUB), SUB), :]


def put_block(ref, field, k, value):
    ref[field, pl.ds(pl.multiple_of(k * SUB, SUB), SUB), :] = value


def pairs_of(n):
    return [(i, j) for i in range(n) for j in range(i, n)]


def lane_sums(slots):
    half, lane = LANES // 2, lane_ids()
    while len(slots) > 1:
        count = len(slots) // 2
        low = (lane & half) == 0
        merged = []
        for one, two in zip(slots[:count], slots[count:]):
            if one is None and two is None:
                merged.append(None)
            elif two is None:
                merged.append(one + roll(one, -half, 1))
            elif one is None:
                merged.append(two + roll(two, half, 1))
            else:
                kept = jnp.where(low, one, two)
                moved = jnp.where(low, roll(one, -half, 1), roll(two, half, 1))
                merged.append(kept + moved)
        slots, half = merged, half // 2
    total = slots[0]
    while half >= 1:
        total = total + roll(total, half, 1)
        half //= 2
    for shift in (4, 2, 1):
        total = total + roll(total, shift, 0)
    return total


def spread(total, lane):
    return jnp.broadcast_to(total[:, lane : lane + 1], (SUB, LANES))


def gathered_total(ref):
    total = ref[0:SUB, :]
    for first in range(SUB, ref.shape[0], SUB):
        total = total + ref[first : first + SUB, :]
    for shift in (4, 2, 1):
        total = total + roll(total, shift, 0)
    return total


def call(kernel, micros, outs, *args, scratch=(), hbm_args=(), hbm_outs=()):
    specs = [
        pl.BlockSpec(memory_space=pltpu.HBM if i in hbm_args else pltpu.VMEM) for i in range(len(args))
    ]
    shapes = [a.shape for i, a in enumerate(args) if i not in hbm_args]
    shapes += [shape for i, shape in enumerate(outs) if i not in hbm_outs]
    shapes += [ref.shape for ref in scratch if ref.memory_space == pltpu.VMEM]
    held = sum(4 * math.prod((*shape[:-1], LANES)) for shape in shapes)
    args = [
        pltpu.with_memory_space_constraint(a, pltpu.HBM) if i in hbm_args else a for i, a in enumerate(args)
    ]
    return pl.pallas_call(
        kernel,
        out_shape=[jax.ShapeDtypeStruct(shape, jnp.float32) for shape in outs],
        in_specs=specs,
        out_specs=[
            pl.BlockSpec(memory_space=pltpu.HBM if i in hbm_outs else pltpu.VMEM) for i in range(len(outs))
        ],
        scratch_shapes=list(scratch),
        compiler_params=pltpu.CompilerParams(vmem_limit_bytes=held + (2 << 20)),
        cost_estimate=pl.CostEstimate(
            flops=0, bytes_accessed=int(micros * 3.5e6), transcendentals=0
        ),
    )(*args)


def sides(width):
    even = lax.rem(lax.axis_index("gx"), 2) == 0
    first = jnp.where(even, width - 1, 0)
    sign = jnp.where(even, 1.0, -1.0)
    return (first, width - 1 - first), (sign, -sign)


def pack_y(fields, first_ref, second_ref, blocks):
    lane = lane_ids()
    even = lax.rem(lax.axis_index("gy"), 2) == 0

    def step(k, carry):
        left = jnp.zeros((SUB, LANES), jnp.float32)
        right = left
        for n, (ref, f) in enumerate(fields):
            value = block(ref, f, k)
            left = jnp.where(lane == (2 * n - 1) % LANES, roll(value, 2 * n - 1, 1), left)
            right = jnp.where(lane == 2 * n, roll(value, 2 * n + 1, 1), right)
        rows = pl.ds(pl.multiple_of(k * SUB, SUB), SUB)
        first_ref[rows, :] = jnp.where(even, right, left)
        second_ref[rows, :] = jnp.where(even, left, right)
        return carry

    lax.fori_loop(0, blocks, step, 0, unroll=4)


def pack_x_kernel(width, sets, q_hbm, base_hbm, q_ref, base_ref, *outs):
    outs, semaphore = outs[:-1], outs[-1]
    layers, _ = sides(width)
    sources, held = (q_hbm, base_hbm), (q_ref, base_ref)
    order = [field for fields in sets for field in fields]
    copies = {
        (which, f): pltpu.make_async_copy(sources[which].at[f], held[which].at[f], semaphore.at[n])
        for n, (which, f) in enumerate(order)
    }
    for copy in copies.values():
        copy.start()
    for fields, pair in zip(sets, zip(outs[::2], outs[1::2])):
        for n, (which, f) in enumerate(fields):
            copies[which, f].wait()
            for out, x in zip(pair, layers):
                out[n] = held[which][f, pl.ds(x, out.shape[1], stride=width), :]


def pack_y_kernel(q_ref, base_ref, first_ref, second_ref):
    fields = [(q_ref, f) for f in range(q_ref.shape[0])]
    fields += [(base_ref, f) for f in range(base_ref.shape[0])]
    pack_y(fields, first_ref, second_ref, q_ref.shape[1] // SUB)


def modes_kernel(width, modes, slot, direct_ref, dual_ref, direct_planes, dual_planes, metric_ref):
    depth = direct_planes.shape[2]
    comps = direct_ref.shape[0] // modes
    layers, _ = sides(width)
    for ref, planes in ((direct_ref, direct_planes), (dual_ref, dual_planes)):
        for f in range(ref.shape[0]):
            for side, x in enumerate(layers):
                planes[side, f] = ref[f, pl.ds(x, depth, stride=width), :]
    todo = pairs_of(modes)
    slots = [None] * LANES

    def step(k, accs):
        accs = list(accs)
        for c in range(comps):
            values = [block(dual_ref, m * comps + c, k) for m in range(modes)]
            for n, (a, b) in enumerate(todo):
                accs[n] = accs[n] + values[a] * values[b]
        return tuple(accs)

    zero = jnp.zeros((SUB, LANES), jnp.float32)
    sums = lax.fori_loop(0, dual_ref.shape[1] // SUB, step, (zero,) * len(todo))
    for n, value in enumerate(sums):
        slots[slot + n] = value
    lane = lane_ids()
    inside = (lane >= slot) & (lane < slot + len(todo))
    metric_ref[...] = jnp.where(inside, lane_sums(slots), 0.0)


def advance_kernel(width, comps, base_at, base_y, projections, *refs):
    q_ref, base_ref, hq_l, hq_r, hb_l, hb_r = refs[:6]
    mode_refs = refs[6 : 6 + projections]
    out_ref, planes_ref, sums_ref = refs[6 + projections :]
    fields, rows = out_ref.shape[:2]
    vectors, blocks = fields // comps, rows // SUB
    depth = rows // width
    lane, row = lane_ids(), row_ids()
    x_at = row % width
    low_x = jnp.where(x_at > 0, 1.0, 0.0)
    high_x = jnp.where(x_at < width - 1, 1.0, 0.0)

    def around(ref, f, k, before, after, halo, lane_at):
        here = block(ref, f, k)
        edge = roll(halo, -lane_at, 1)
        y_low = jnp.where(lane == 0, edge, roll(here, 1, 1))
        y_high = jnp.where(lane == LANES - 1, edge, roll(here, -1, 1))
        x_low, x_high = roll(here, 1, 0), roll(here, -1, 0)
        z_low, z_high = z_neighbours(here, block(ref, f, before), block(ref, f, after))
        return here, (x_low, y_low, z_low), (x_high, y_high, z_high)

    def z_neighbours(here, earlier, later):
        shift = SUB - width
        if shift == 0:
            return earlier, later
        low = roll(jnp.where(row < SUB - width, here, earlier), width, 0)
        high = roll(jnp.where(row < width, later, here), -width, 0)
        return low, high

    def step(k, carry):
        before = lax.rem(k + blocks - 1, blocks)
        after = lax.rem(k + 1, blocks)
        rows_k = pl.ds(pl.multiple_of(k * SUB, SUB), SUB)
        halo_q = hq_l[rows_k, :] + hq_r[rows_k, :]
        halo_b = hb_l[rows_k, :] + hb_r[rows_k, :]
        centre, grads = [], []
        for j in range(comps):
            here, low, high = around(base_ref, base_at + j, k, before, after, halo_b, 2 * (base_y + j))
            centre.append(HALF * here)
            grads.append(
                (
                    HALF * (high[0] * high_x - low[0] * low_x),
                    HALF * (high[1] - low[1]),
                    HALF * (high[2] - low[2]),
                )
            )
        plus = [(DIFF + centre[0]) * high_x, DIFF + centre[1], DIFF + centre[2]]
        minus = [(DIFF - centre[0]) * low_x, DIFF - centre[1], DIFF - centre[2]]
        for v in range(vectors):
            values = []
            sums = []
            for c in range(comps):
                f = v * comps + c
                here, low, high = around(
                    q_ref, f, k, before, after, halo_q, 2 * f
                )
                total = (1.0 - 6.0 * DIFF) * here
                for d in range(3):
                    total = total + plus[d] * high[d] + minus[d] * low[d]
                values.append(here)
                sums.append(total)
            for c in range(comps):
                total = sums[c]
                for j in range(comps):
                    total = total - values[j] * grads[j][c]
                put_block(out_ref, v * comps + c, k, total)
        return carry

    lax.fori_loop(0, blocks, step, 0)
    layers, _ = sides(width)
    for f in range(fields):
        for side, x in enumerate(layers):
            planes_ref[side, f] = out_ref[f, pl.ds(x, depth, stride=width), :]

    zero = jnp.zeros((SUB, LANES), jnp.float32)
    at = 0
    for ref in mode_refs:
        modes = ref.shape[0] // comps

        def dots(k, accs):
            accs = list(accs)
            for c in range(comps):
                right = [block(out_ref, v * comps + c, k) for v in range(vectors)]
                for m in range(modes):
                    left = block(ref, m * comps + c, k)
                    for v in range(vectors):
                        accs[m * vectors + v] = accs[m * vectors + v] + left * right[v]
            return tuple(accs)

        for value in lax.fori_loop(0, blocks, dots, (zero,) * (modes * vectors)):
            sums_ref[at] = value
            at += 1
    if sums_ref.shape[0] > at:
        keep = (x_at > 0) & (x_at < width - 1)
        own = pairs_of(vectors)

        def gram(k, accs):
            accs = list(accs)
            for c in range(comps):
                inner = [jnp.where(keep, block(out_ref, v * comps + c, k), 0.0) for v in range(vectors)]
                for n, (i, j) in enumerate(own):
                    accs[n] = accs[n] + inner[i] * inner[j]
            return tuple(accs)

        for value in lax.fori_loop(0, blocks, gram, (zero,) * len(own)):
            sums_ref[at] = value
            at += 1


def edge_kernel(width, comps, side, at, lanes, projections, extra, *refs):
    own_q, own_b, halo_q, halo_b, advanced, sums_ref = refs[:6]
    mode_refs, refs = refs[6 : 6 + projections], refs[6 + projections :]
    extra_refs, (new_ref, result_ref) = refs[:extra], refs[extra:]
    fields, depth = new_ref.shape[:2]
    vectors, blocks = fields // comps, depth // SUB
    scale = sides(width)[1][side] * HALF

    def step(k, carry):
        rows = pl.ds(pl.multiple_of(k * SUB, SUB), SUB)
        factor = DIFF + scale * own_b[at[0], rows, :]
        outer = [scale * halo_b[at[1] + j, rows, :] for j in range(comps)]
        for v in range(vectors):
            for c in range(comps):
                value = factor * halo_q[v * comps + c, rows, :]
                if c == 0:
                    for j in range(comps):
                        value = value - own_q[v * comps + j, rows, :] * outer[j]
                new_ref[v * comps + c, rows, :] = value
        return carry

    lax.fori_loop(0, blocks, step, 0)
    total = []
    for ref in mode_refs:
        modes = ref.shape[1] // comps
        accs = tuple(sums_ref[len(total) + i] for i in range(modes * vectors))

        def dots(k, accs, ref=ref):
            accs = list(accs)
            rows = pl.ds(pl.multiple_of(k * SUB, SUB), SUB)
            for c in range(comps):
                right = [new_ref[v * comps + c, rows, :] for v in range(vectors)]
                for m in range(modes):
                    left = ref[side, m * comps + c, rows, :]
                    for v in range(vectors):
                        accs[m * vectors + v] = accs[m * vectors + v] + left * right[v]
            return tuple(accs)

        total += lax.fori_loop(0, blocks, dots, accs)
    own = pairs_of(vectors)
    squares = len(total) < sums_ref.shape[0]
    accs = tuple(sums_ref[len(total) + i] for i in range(len(own))) if squares else ()

    def finish(k, accs):
        accs = list(accs)
        rows = pl.ds(pl.multiple_of(k * SUB, SUB), SUB)
        for c in range(comps):
            inner = []
            for v in range(vectors):
                f = v * comps + c
                inner.append(new_ref[f, rows, :] + advanced[side, f, rows, :])
                new_ref[f, rows, :] = inner[v]
            if squares:
                for n, (i, j) in enumerate(own):
                    accs[n] = accs[n] + inner[i] * inner[j]
        return tuple(accs)

    total += lax.fori_loop(0, blocks, finish, accs)
    if lanes is None:
        for n, value in enumerate(total):
            result_ref[n] = value
        return
    slots = dict(zip(lanes, total))
    lane = lane_ids()
    inside = lane < 0
    for position in slots:
        inside = inside | (lane == position)
    packed = jnp.where(inside, lane_sums([slots.get(i) for i in range(LANES)]), 0.0)
    for ref in extra_refs:
        packed = packed + ref[...]
    for first in range(0, result_ref.shape[0], SUB):
        result_ref[first : first + SUB, :] = packed


def edges(width, comps, at, lanes, micros, devices, own_q, own_b, halo_q, halo_b, advanced, sums, modes, extra):
    layers = []
    for side in range(2):
        last = side == 1
        kernel = functools.partial(
            edge_kernel, width, comps, side, at, lanes if last else None, len(modes), len(extra) if last else 0
        )
        new, sums = call(
            kernel,
            micros,
            [advanced.shape[1:], (devices, LANES) if last else sums.shape],
            own_q[side],
            own_b[side],
            halo_q[side],
            halo_b[side],
            advanced,
            sums,
            *modes,
            *(extra if last else ()),
        )
        layers.append(new)
    return layers, sums


def deflate_planes_kernel(comps, lanes, side, gathered, planes, dual_planes, out, factors):
    total = gathered_total(gathered)
    for i, lane in enumerate(lanes):
        factors[i] = spread(total, lane)
    fields, depth = out.shape[:2]
    vectors = fields // comps
    modes = dual_planes.shape[1] // comps

    def step(k, carry):
        rows = pl.ds(pl.multiple_of(k * SUB, SUB), SUB)
        for c in range(comps):
            values = [planes[v * comps + c, rows, :] for v in range(vectors)]
            for m in range(modes):
                mode = dual_planes[side, m * comps + c, rows, :]
                for v in range(vectors):
                    values[v] = values[v] - factors[m * vectors + v] * mode
            for v in range(vectors):
                out[v * comps + c, rows, :] = values[v]
        return carry

    lax.fori_loop(0, depth // SUB, step, 0)


def deflate_kernel(
    width, comps, lanes, gathered, advanced, dual, planes_a, planes_b, out_ref, first_ref, second_ref, factors
):
    total = gathered_total(gathered)
    for i, lane in enumerate(lanes):
        factors[i] = spread(total, lane)
    fields, rows_all = out_ref.shape[:2]
    vectors = fields // comps
    modes = dual.shape[0] // comps

    def step(k, carry):
        for c in range(comps):
            values = [block(advanced, v * comps + c, k) for v in range(vectors)]
            for m in range(modes):
                mode = block(dual, m * comps + c, k)
                for v in range(vectors):
                    values[v] = values[v] - factors[m * vectors + v] * mode
            for v in range(vectors):
                put_block(out_ref, v * comps + c, k, values[v])
        return carry

    lax.fori_loop(0, rows_all // SUB, step, 0)
    depth = rows_all // width
    layers, _ = sides(width)
    for f in range(fields):
        for planes, x in zip((planes_a, planes_b), layers):
            out_ref[f, pl.ds(x, depth, stride=width), :] = planes[f]
    pack_y([(out_ref, f) for f in range(fields)], first_ref, second_ref, rows_all // SUB)


def finish_kernel(width, comps, layout, scale, *refs):
    gathered, dual, advanced, *planes, out_hbm, growth_ref, out_ref, factors, semaphore = refs
    fields, rows_all = out_ref.shape[:2]
    vectors, modes = fields // comps, dual.shape[0] // comps
    depth = rows_all // width
    layers, _ = sides(width)
    total = gathered_total(gathered)
    first, cross, self_gram, metric = layout
    coef = {key: spread(total, lane) for key, lane in first.items()}
    mixed = {key: spread(total, lane) for key, lane in cross.items()}
    inner = {key: spread(total, lane) for key, lane in self_gram.items()}
    weight = {key: spread(total, lane) for key, lane in metric.items()}
    weighted = {}
    for m in range(modes):
        for j in range(vectors):
            weighted[m, j] = sum(weight[min(m, n), max(m, n)] * coef[n, j] for n in range(modes))
    gram = {}
    for i, j in pairs_of(vectors):
        value = inner[i, j]
        for m in range(modes):
            value = value - coef[m, i] * (mixed[m, j] - weighted[m, j]) - coef[m, j] * mixed[m, i]
        gram[j, i] = value
    lower, inverse_diagonal = {}, {}
    for j in range(vectors):
        value = gram[j, j]
        for n in range(j):
            value = value - lower[j, n] * lower[j, n]
        lower[j, j] = jnp.sqrt(value)
        inverse_diagonal[j] = 1.0 / lower[j, j]
        for i in range(j + 1, vectors):
            value = gram[i, j]
            for n in range(j):
                value = value - lower[i, n] * lower[j, n]
            lower[i, j] = value * inverse_diagonal[j]
    inverse = {}
    for j in range(vectors):
        inverse[j, j] = inverse_diagonal[j]
        for i in range(j + 1, vectors):
            value = sum(lower[i, n] * inverse[n, j] for n in range(j, i))
            inverse[i, j] = -inverse_diagonal[i] * value
    row, lane = row_ids(), lane_ids()
    growth = jnp.zeros((SUB, LANES), jnp.float32)
    for (i, j), value in lower.items():
        growth = jnp.where((row == i) & (lane == j), value, growth)
    growth_ref[...] = growth[:vectors, :vectors]
    at = {}
    for (i, j), value in inverse.items():
        at[i, j] = len(at)
        factors[at[i, j]] = scale * value
    mode_at = {}
    for i in range(vectors):
        for m in range(modes):
            mode_at[i, m] = len(at) + len(mode_at)
            factors[mode_at[i, m]] = -scale * sum(inverse[i, j] * coef[m, j] for j in range(i + 1))
    for f in range(fields):
        for own, x in zip(planes, layers):
            out_ref[f, pl.ds(x, depth, stride=width), :] = own[f]
    outer = (row % width == 0) | (row % width == width - 1)

    def step(k, carry):
        for c in range(comps):
            parts = []
            for v in range(vectors):
                inner = block(advanced, v * comps + c, k)
                parts.append(jnp.where(outer, block(out_ref, v * comps + c, k), inner))
            values = []
            for i in range(vectors):
                value = factors[at[i, 0]] * parts[0]
                for j in range(1, i + 1):
                    value = value + factors[at[i, j]] * parts[j]
                values.append(value)
            for m in range(modes):
                mode = block(dual, m * comps + c, k)
                for i in range(vectors):
                    values[i] = values[i] + factors[mode_at[i, m]] * mode
            for i in range(vectors):
                put_block(out_ref, i * comps + c, k, values[i])
        return carry

    chunks = semaphore.shape[0]
    size = rows_all // SUB // chunks
    copies = []
    for n in range(chunks):
        lax.fori_loop(n * size, (n + 1) * size, step, 0)
        rows = pl.ds(n * size * SUB, size * SUB)
        copy = pltpu.make_async_copy(out_ref.at[:, rows], out_hbm.at[:, rows], semaphore.at[n])
        copy.start()
        copies.append(copy)
    for copy in copies:
        copy.wait()


def swap(first, second, axis):
    count = lax.axis_size(axis)
    results = []
    for field, start in ((first, 0), (second, 1)):
        pairs = [(i, i + 1) for i in range(start, count - 1, 2)]
        results.append(lax.ppermute(field, axis, pairs + [(j, i) for i, j in pairs]))
    return results


def exchange(payload):
    return lax.all_to_all(payload, ("gx", "gy"), 0, 0, tiled=True)


def body(adjoint_block, base_flow, direct_modes, dual_modes):
    vectors, comps, depth, width, length = adjoint_block.shape
    steps, modes = base_flow.shape[0], direct_modes.shape[0]
    rows = depth * width
    assert length == LANES and SUB % width == 0 and rows % SUB == 0 and depth % SUB == 0
    devices = lax.axis_size("gx") * lax.axis_size("gy")
    cells = float(comps * rows * length * devices)
    fields = vectors * comps

    q = adjoint_block.reshape(fields, rows, length)
    base = base_flow.reshape(steps * comps, rows, length)
    direct = direct_modes.reshape(modes * comps, rows, length)
    dual = dual_modes.reshape(modes * comps, rows, length)
    plane = (depth, length)

    sets = [
        [(0, f) for f in range(fields)] + [(1, j) for j in range(comps)],
        [(1, comps + j) for j in range(comps)],
    ]
    q, base, *layers, late_a, late_b = call(
        functools.partial(pack_x_kernel, width, sets),
        1.5,
        [q.shape, base.shape] + [(len(some), *plane) for some in sets for _ in range(2)],
        q,
        base,
        scratch=[pltpu.SemaphoreType.DMA((fields + steps * comps,))],
        hbm_args=(0, 1),
    )
    halo_x = swap(*layers, "gx")
    halo_late = swap(late_a, late_b, "gx")
    halo_y = swap(*call(pack_y_kernel, 3, [(rows, LANES)] * 2, q, base), "gy")

    pairs, mode_pairs = pairs_of(vectors), pairs_of(modes)
    first = {(m, i): m * vectors + i for m in range(modes) for i in range(vectors)}
    cross = {key: modes * vectors + lane for key, lane in first.items()}
    self_gram = {key: 2 * modes * vectors + n for n, key in enumerate(pairs)}
    slot = 2 * modes * vectors + len(pairs)
    metric = {key: slot + n for n, key in enumerate(mode_pairs)}
    assert slot + len(mode_pairs) <= LANES
    direct_planes, dual_planes, metric_part = call(
        functools.partial(modes_kernel, width, modes, slot),
        4,
        [(2, modes * comps, *plane)] * 2 + [(SUB, LANES)],
        direct,
        dual,
    )

    spacing = LANES // (1 << (modes * vectors - 1).bit_length())
    spaced = [spacing * n for n in range(modes * vectors)]
    advanced, planes, sums = call(
        functools.partial(advance_kernel, width, comps, 0, fields, 1),
        5,
        [(fields, rows, length), (2, fields, *plane), (modes * vectors, SUB, LANES)],
        q,
        base,
        *halo_y,
        *halo_y,
        direct,
    )
    edge, payload = edges(
        width,
        comps,
        (fields, fields),
        spaced,
        0.9,
        devices,
        layers,
        layers,
        halo_x,
        halo_x,
        planes,
        sums,
        [direct_planes],
        [],
    )
    gathered = exchange(payload)

    scratch = [pltpu.VMEM((modes * vectors, SUB, LANES), jnp.float32)]
    layers = [
        call(
            functools.partial(deflate_planes_kernel, comps, spaced, side),
            0.6,
            [(fields, *plane)],
            gathered,
            edge[side],
            dual_planes,
            scratch=scratch,
        )[0]
        for side in range(2)
    ]
    halo_x = swap(*layers, "gx")
    current, *columns = call(
        functools.partial(deflate_kernel, width, comps, spaced),
        3,
        [(fields, rows, length), (rows, LANES), (rows, LANES)],
        gathered,
        advanced,
        dual,
        *layers,
        scratch=scratch,
    )
    columns = swap(*columns, "gy")
    advanced, planes, sums = call(
        functools.partial(advance_kernel, width, comps, comps, fields + comps, 2),
        12,
        [(fields, rows, length), (2, fields, *plane), (2 * modes * vectors + len(pairs), SUB, LANES)],
        current,
        base,
        *columns,
        *halo_y,
        direct,
        dual,
    )
    lanes = list(first.values()) + list(cross.values()) + list(self_gram.values())
    edge, payload = edges(
        width,
        comps,
        (0, 0),
        lanes,
        1.3,
        devices,
        layers,
        (late_a, late_b),
        halo_x,
        halo_late,
        planes,
        sums,
        [direct_planes, dual_planes],
        [metric_part],
    )
    total = exchange(payload)
    factor_count = vectors * (vectors + 1) // 2 + modes * vectors
    chunks = math.gcd(rows // SUB, 4)
    next_block, growth = call(
        functools.partial(finish_kernel, width, comps, (first, cross, self_gram, metric), math.sqrt(cells)),
        3,
        [(fields, rows, length), (vectors, vectors)],
        total,
        dual,
        advanced,
        *edge,
        scratch=[
            pltpu.VMEM((fields, rows, length), jnp.float32),
            pltpu.VMEM((factor_count, SUB, LANES), jnp.float32),
            pltpu.SemaphoreType.DMA((chunks,)),
        ],
        hbm_outs=(0,),
    )
    return (next_block.reshape(adjoint_block.shape), growth)


def solution(mesh):
    placed = P(None, None, None, "gx", "gy")
    return jax.shard_map(
        body,
        mesh=mesh,
        in_specs=(placed,) * 4,
        out_specs=(placed, P()),
        check_vma=False,
    )
```

```python
import functools
import math

import jax
import jax.numpy as jnp
from jax import lax
from jax.experimental import pallas as pl
from jax.experimental.pallas import tpu as pltpu
from jax.sharding import PartitionSpec as P


step_size = 0.1
viscosity = 0.2
HALF = 0.5 * step_size
DIFF = step_size * viscosity
SUB = 8
LANES = 128


def lane_ids():
    return lax.broadcasted_iota(jnp.int32, (SUB, LANES), 1)


def row_ids():
    return lax.broadcasted_iota(jnp.int32, (SUB, LANES), 0)


def roll(x, shift, axis):
    shift %= x.shape[axis]
    return x if shift == 0 else pltpu.roll(x, shift, axis)


def block(ref, field, k):
    return ref[field, pl.ds(pl.multiple_of(k * SUB, SUB), SUB), :]


def put_block(ref, field, k, value):
    ref[field, pl.ds(pl.multiple_of(k * SUB, SUB), SUB), :] = value


def pairs_of(n):
    return [(i, j) for i in range(n) for j in range(i, n)]


def lane_sums(slots):
    half, lane = LANES // 2, lane_ids()
    while len(slots) > 1:
        count = len(slots) // 2
        low = (lane & half) == 0
        merged = []
        for one, two in zip(slots[:count], slots[count:]):
            if one is None and two is None:
                merged.append(None)
            elif two is None:
                merged.append(one + roll(one, -half, 1))
            elif one is None:
                merged.append(two + roll(two, half, 1))
            else:
                kept = jnp.where(low, one, two)
                moved = jnp.where(low, roll(one, -half, 1), roll(two, half, 1))
                merged.append(kept + moved)
        slots, half = merged, half // 2
    total = slots[0]
    while half >= 1:
        total = total + roll(total, half, 1)
        half //= 2
    for shift in (4, 2, 1):
        total = total + roll(total, shift, 0)
    return total


def spread(total, lane):
    return jnp.broadcast_to(total[:, lane : lane + 1], (SUB, LANES))


def gathered_total(ref):
    total = ref[0:SUB, :]
    for first in range(SUB, ref.shape[0], SUB):
        total = total + ref[first : first + SUB, :]
    for shift in (4, 2, 1):
        total = total + roll(total, shift, 0)
    return total


def call(kernel, micros, outs, *args, scratch=(), hbm_args=(), hbm_outs=()):
    specs = [
        pl.BlockSpec(memory_space=pltpu.HBM if i in hbm_args else pltpu.VMEM) for i in range(len(args))
    ]
    shapes = [a.shape for i, a in enumerate(args) if i not in hbm_args]
    shapes += [shape for i, shape in enumerate(outs) if i not in hbm_outs]
    shapes += [ref.shape for ref in scratch if ref.memory_space == pltpu.VMEM]
    held = sum(4 * math.prod((*shape[:-1], LANES)) for shape in shapes)
    args = [
        pltpu.with_memory_space_constraint(a, pltpu.HBM) if i in hbm_args else a for i, a in enumerate(args)
    ]
    return pl.pallas_call(
        kernel,
        out_shape=[jax.ShapeDtypeStruct(shape, jnp.float32) for shape in outs],
        in_specs=specs,
        out_specs=[
            pl.BlockSpec(memory_space=pltpu.HBM if i in hbm_outs else pltpu.VMEM) for i in range(len(outs))
        ],
        scratch_shapes=list(scratch),
        compiler_params=pltpu.CompilerParams(vmem_limit_bytes=held + (2 << 20)),
        cost_estimate=pl.CostEstimate(
            flops=0, bytes_accessed=int(micros * 3.5e6), transcendentals=0
        ),
    )(*args)


def sides(width):
    even = lax.rem(lax.axis_index("gx"), 2) == 0
    first = jnp.where(even, width - 1, 0)
    sign = jnp.where(even, 1.0, -1.0)
    return (first, width - 1 - first), (sign, -sign)


def pack_y(fields, first_ref, second_ref, blocks):
    lane = lane_ids()
    even = lax.rem(lax.axis_index("gy"), 2) == 0

    def step(k, carry):
        left = jnp.zeros((SUB, LANES), jnp.float32)
        right = left
        for n, (ref, f) in enumerate(fields):
            value = block(ref, f, k)
            left = jnp.where(lane == (2 * n - 1) % LANES, roll(value, 2 * n - 1, 1), left)
            right = jnp.where(lane == 2 * n, roll(value, 2 * n + 1, 1), right)
        rows = pl.ds(pl.multiple_of(k * SUB, SUB), SUB)
        first_ref[rows, :] = jnp.where(even, right, left)
        second_ref[rows, :] = jnp.where(even, left, right)
        return carry

    lax.fori_loop(0, blocks, step, 0, unroll=4)


def pack_x_kernel(width, sets, q_hbm, base_hbm, q_ref, base_ref, *outs):
    outs, semaphore = outs[:-1], outs[-1]
    layers, _ = sides(width)
    sources, held = (q_hbm, base_hbm), (q_ref, base_ref)
    order = [field for fields in sets for field in fields]
    copies = {
        (which, f): pltpu.make_async_copy(sources[which].at[f], held[which].at[f], semaphore.at[n])
        for n, (which, f) in enumerate(order)
    }
    for copy in copies.values():
        copy.start()
    for fields, pair in zip(sets, zip(outs[::2], outs[1::2])):
        for n, (which, f) in enumerate(fields):
            copies[which, f].wait()
            for out, x in zip(pair, layers):
                out[n] = held[which][f, pl.ds(x, out.shape[1], stride=width), :]


def pack_y_kernel(q_ref, base_ref, first_ref, second_ref):
    fields = [(q_ref, f) for f in range(q_ref.shape[0])]
    fields += [(base_ref, f) for f in range(base_ref.shape[0])]
    pack_y(fields, first_ref, second_ref, q_ref.shape[1] // SUB)


def modes_kernel(
    width, modes, slot, direct_hbm, dual_hbm, direct_ref, dual_ref, direct_planes, dual_planes, metric_ref, semaphore
):
    depth = direct_planes.shape[2]
    comps = direct_ref.shape[0] // modes
    layers, _ = sides(width)
    parts = ((dual_hbm, dual_ref, dual_planes), (direct_hbm, direct_ref, direct_planes))
    copies = []
    for n, (source, ref, _) in enumerate(parts):
        for f in range(modes * comps):
            copies.append(pltpu.make_async_copy(source.at[f], ref.at[f], semaphore.at[n, f]))
            copies[-1].start()
    for n, (_, ref, planes) in enumerate(parts):
        for f in range(modes * comps):
            copies[n * modes * comps + f].wait()
            for side, x in enumerate(layers):
                planes[side, f] = ref[f, pl.ds(x, depth, stride=width), :]
    todo = pairs_of(modes)
    slots = [None] * LANES

    def step(k, accs):
        accs = list(accs)
        for c in range(comps):
            values = [block(dual_ref, m * comps + c, k) for m in range(modes)]
            for n, (a, b) in enumerate(todo):
                accs[n] = accs[n] + values[a] * values[b]
        return tuple(accs)

    zero = jnp.zeros((SUB, LANES), jnp.float32)
    sums = lax.fori_loop(0, dual_ref.shape[1] // SUB, step, (zero,) * len(todo))
    for n, value in enumerate(sums):
        slots[slot + n] = value
    lane = lane_ids()
    inside = (lane >= slot) & (lane < slot + len(todo))
    metric_ref[...] = jnp.where(inside, lane_sums(slots), 0.0)


def advance_kernel(width, comps, base_at, base_y, projections, *refs):
    q_ref, base_ref, hq_l, hq_r, hb_l, hb_r = refs[:6]
    mode_refs = refs[6 : 6 + projections]
    out_ref, planes_ref, sums_ref = refs[6 + projections :]
    fields, rows = out_ref.shape[:2]
    vectors, blocks = fields // comps, rows // SUB
    depth = rows // width
    lane, row = lane_ids(), row_ids()
    x_at = row % width
    low_x = jnp.where(x_at > 0, 1.0, 0.0)
    high_x = jnp.where(x_at < width - 1, 1.0, 0.0)
    upper = row < width

    def around(ref, f, k, before, after, halo, lane_at):
        here = block(ref, f, k)
        edge = roll(halo, -lane_at, 1)
        y_low = jnp.where(lane == 0, edge, roll(here, 1, 1))
        y_high = jnp.where(lane == LANES - 1, edge, roll(here, -1, 1))
        x_low, x_high = roll(here, 1, 0), roll(here, -1, 0)
        z_low, z_high = z_neighbours(here, block(ref, f, before), block(ref, f, after))
        return here, (x_low, y_low, z_low), (x_high, y_high, z_high)

    def z_neighbours(here, earlier, later):
        shift = SUB - width
        if shift == 0:
            return earlier, later
        low = roll(jnp.where(row < SUB - width, here, earlier), width, 0)
        high = roll(jnp.where(row < width, later, here), -width, 0)
        return low, high

    def step(k, carry):
        before = lax.rem(k + blocks - 1, blocks)
        after = lax.rem(k + 1, blocks)
        rows_k = pl.ds(pl.multiple_of(k * SUB, SUB), SUB)
        halo_q = hq_l[rows_k, :] + hq_r[rows_k, :]
        halo_b = hb_l[rows_k, :] + hb_r[rows_k, :]
        centre, grads = [], []
        for j in range(comps):
            here, low, high = around(base_ref, base_at + j, k, before, after, halo_b, 2 * (base_y + j))
            centre.append(HALF * here)
            grads.append(
                (
                    HALF * (high[0] * high_x - low[0] * low_x),
                    HALF * (high[1] - low[1]),
                    HALF * (high[2] - low[2]),
                )
            )
        plus = [(DIFF + centre[0]) * high_x, DIFF + centre[1], DIFF + centre[2]]
        minus = [(DIFF - centre[0]) * low_x, DIFF - centre[1], DIFF - centre[2]]
        for v in range(vectors):
            values = []
            sums = []
            for c in range(comps):
                f = v * comps + c
                here, low, high = around(
                    q_ref, f, k, before, after, halo_q, 2 * f
                )
                total = (1.0 - 6.0 * DIFF) * here
                for d in range(3):
                    total = total + plus[d] * high[d] + minus[d] * low[d]
                values.append(here)
                sums.append(total)
            for c in range(comps):
                total = sums[c]
                for j in range(comps):
                    total = total - values[j] * grads[j][c]
                put_block(out_ref, v * comps + c, k, total)
        return carry

    lax.fori_loop(0, blocks, step, 0)
    layers, _ = sides(width)
    for f in range(fields):
        for side, x in enumerate(layers):
            planes_ref[side, f] = out_ref[f, pl.ds(x, depth, stride=width), :]

    zero = jnp.zeros((SUB, LANES), jnp.float32)
    at = 0
    for ref in mode_refs:
        modes = ref.shape[0] // comps

        def dots(k, accs):
            accs = list(accs)
            for c in range(comps):
                right = [block(out_ref, v * comps + c, k) for v in range(vectors)]
                for m in range(modes):
                    left = block(ref, m * comps + c, k)
                    for v in range(vectors):
                        accs[m * vectors + v] = accs[m * vectors + v] + left * right[v]
            return tuple(accs)

        for value in lax.fori_loop(0, blocks, dots, (zero,) * (modes * vectors)):
            sums_ref[at] = value
            at += 1
    if sums_ref.shape[0] > at:
        keep = (x_at > 0) & (x_at < width - 1)
        own = pairs_of(vectors)

        def gram(k, accs):
            accs = list(accs)
            for c in range(comps):
                inner = [jnp.where(keep, block(out_ref, v * comps + c, k), 0.0) for v in range(vectors)]
                for n, (i, j) in enumerate(own):
                    accs[n] = accs[n] + inner[i] * inner[j]
            return tuple(accs)

        for value in lax.fori_loop(0, blocks, gram, (zero,) * len(own)):
            sums_ref[at] = value
            at += 1


def edge_kernel(width, comps, at, lanes, projections, extra, *refs):
    own_q, own_b, halo_q, halo_b = (refs[n : n + 2] for n in (0, 2, 4, 6))
    advanced, sums_ref = refs[8:10]
    mode_refs, refs = refs[10 : 10 + projections], refs[10 + projections :]
    extra_refs, (new_a, new_b, payload_ref) = refs[:extra], refs[extra:]
    new_refs = (new_a, new_b)
    fields, depth = new_a.shape[:2]
    vectors, blocks = fields // comps, depth // SUB
    _, signs = sides(width)

    def step(k, carry):
        rows = pl.ds(pl.multiple_of(k * SUB, SUB), SUB)
        for side in range(2):
            scale = signs[side] * HALF
            factor = DIFF + scale * own_b[side][at[0], rows, :]
            outer = [scale * halo_b[side][at[1] + j, rows, :] for j in range(comps)]
            for v in range(vectors):
                for c in range(comps):
                    value = factor * halo_q[side][v * comps + c, rows, :]
                    if c == 0:
                        for j in range(comps):
                            value = value - own_q[side][v * comps + j, rows, :] * outer[j]
                    new_refs[side][v * comps + c, rows, :] = value
        return carry

    lax.fori_loop(0, blocks, step, 0)
    total = []
    for ref in mode_refs:
        modes = ref.shape[1] // comps
        accs = tuple(sums_ref[len(total) + i] for i in range(modes * vectors))

        def dots(k, accs, ref=ref):
            accs = list(accs)
            rows = pl.ds(pl.multiple_of(k * SUB, SUB), SUB)
            for side in range(2):
                for c in range(comps):
                    right = [new_refs[side][v * comps + c, rows, :] for v in range(vectors)]
                    for m in range(modes):
                        left = ref[side, m * comps + c, rows, :]
                        for v in range(vectors):
                            accs[m * vectors + v] = accs[m * vectors + v] + left * right[v]
            return tuple(accs)

        total += lax.fori_loop(0, blocks, dots, accs)
    own = pairs_of(vectors)
    squares = len(total) < sums_ref.shape[0]
    accs = tuple(sums_ref[len(total) + i] for i in range(len(own))) if squares else ()

    def finish(k, accs):
        accs = list(accs)
        rows = pl.ds(pl.multiple_of(k * SUB, SUB), SUB)
        for side in range(2):
            for c in range(comps):
                inner = []
                for v in range(vectors):
                    f = v * comps + c
                    inner.append(new_refs[side][f, rows, :] + advanced[side, f, rows, :])
                    new_refs[side][f, rows, :] = inner[v]
                if squares:
                    for n, (i, j) in enumerate(own):
                        accs[n] = accs[n] + inner[i] * inner[j]
        return tuple(accs)

    total += lax.fori_loop(0, blocks, finish, accs)
    slots = dict(zip(lanes, total))
    lane = lane_ids()
    inside = lane < 0
    for position in slots:
        inside = inside | (lane == position)
    packed = jnp.where(inside, lane_sums([slots.get(i) for i in range(LANES)]), 0.0)
    for ref in extra_refs:
        packed = packed + ref[...]
    for first in range(0, payload_ref.shape[0], SUB):
        payload_ref[first : first + SUB, :] = packed


def edges(width, comps, at, lanes, micros, devices, own_q, own_b, halo_q, halo_b, advanced, sums, modes, extra):
    kernel = functools.partial(edge_kernel, width, comps, at, lanes, len(modes), len(extra))
    shapes = [advanced.shape[1:], advanced.shape[1:], (devices, LANES)]
    args = (*own_q, *own_b, *halo_q, *halo_b, advanced, sums, *modes, *extra)
    *layers, payload = call(kernel, micros, shapes, *args)
    return layers, payload


def deflate_planes_kernel(comps, lanes, gathered, plane_a, plane_b, late_a, late_b, dual_planes, out_a, out_b, factors):
    total = gathered_total(gathered)
    for i, lane in enumerate(lanes):
        factors[i] = spread(total, lane)
    fields, depth = plane_a.shape[:2]
    vectors = fields // comps
    modes = dual_planes.shape[1] // comps
    for late, out in ((late_a, out_a), (late_b, out_b)):
        for j in range(comps):
            out[fields + j] = late[j]

    def step(k, carry):
        rows = pl.ds(pl.multiple_of(k * SUB, SUB), SUB)
        for side, (plane, out) in enumerate(((plane_a, out_a), (plane_b, out_b))):
            for c in range(comps):
                values = [plane[v * comps + c, rows, :] for v in range(vectors)]
                for m in range(modes):
                    mode = dual_planes[side, m * comps + c, rows, :]
                    for v in range(vectors):
                        values[v] = values[v] - factors[m * vectors + v] * mode
                for v in range(vectors):
                    out[v * comps + c, rows, :] = values[v]
        return carry

    lax.fori_loop(0, depth // SUB, step, 0)


def deflate_kernel(
    width, comps, lanes, gathered, advanced, dual, planes_a, planes_b, out_ref, first_ref, second_ref, factors
):
    total = gathered_total(gathered)
    for i, lane in enumerate(lanes):
        factors[i] = spread(total, lane)
    fields, rows_all = out_ref.shape[:2]
    vectors = fields // comps
    modes = dual.shape[0] // comps

    def step(k, carry):
        for c in range(comps):
            values = [block(advanced, v * comps + c, k) for v in range(vectors)]
            for m in range(modes):
                mode = block(dual, m * comps + c, k)
                for v in range(vectors):
                    values[v] = values[v] - factors[m * vectors + v] * mode
            for v in range(vectors):
                put_block(out_ref, v * comps + c, k, values[v])
        return carry

    lax.fori_loop(0, rows_all // SUB, step, 0)
    depth = rows_all // width
    layers, _ = sides(width)
    for f in range(fields):
        for planes, x in zip((planes_a, planes_b), layers):
            out_ref[f, pl.ds(x, depth, stride=width), :] = planes[f]
    pack_y([(out_ref, f) for f in range(fields)], first_ref, second_ref, rows_all // SUB)


def finish_kernel(width, comps, layout, scale, *refs):
    gathered, dual, advanced, *planes, out_hbm, growth_hbm, out_ref, growth_ref, factors, semaphore = refs
    fields, rows_all = out_ref.shape[:2]
    vectors, modes = fields // comps, dual.shape[0] // comps
    depth = rows_all // width
    layers, _ = sides(width)
    total = gathered_total(gathered)
    first, cross, self_gram, metric = layout
    coef = {key: spread(total, lane) for key, lane in first.items()}
    mixed = {key: spread(total, lane) for key, lane in cross.items()}
    inner = {key: spread(total, lane) for key, lane in self_gram.items()}
    weight = {key: spread(total, lane) for key, lane in metric.items()}
    weighted = {}
    for m in range(modes):
        for j in range(vectors):
            weighted[m, j] = sum(weight[min(m, n), max(m, n)] * coef[n, j] for n in range(modes))
    gram = {}
    for i, j in pairs_of(vectors):
        value = inner[i, j]
        for m in range(modes):
            value = value - coef[m, i] * (mixed[m, j] - weighted[m, j]) - coef[m, j] * mixed[m, i]
        gram[j, i] = value
    lower, inverse_diagonal = {}, {}
    for j in range(vectors):
        value = gram[j, j]
        for n in range(j):
            value = value - lower[j, n] * lower[j, n]
        lower[j, j] = jnp.sqrt(value)
        inverse_diagonal[j] = 1.0 / lower[j, j]
        for i in range(j + 1, vectors):
            value = gram[i, j]
            for n in range(j):
                value = value - lower[i, n] * lower[j, n]
            lower[i, j] = value * inverse_diagonal[j]
    inverse = {}
    for j in range(vectors):
        inverse[j, j] = inverse_diagonal[j]
        for i in range(j + 1, vectors):
            value = sum(lower[i, n] * inverse[n, j] for n in range(j, i))
            inverse[i, j] = -inverse_diagonal[i] * value
    row, lane = row_ids(), lane_ids()
    growth = jnp.zeros((SUB, LANES), jnp.float32)
    for (i, j), value in lower.items():
        growth = jnp.where((row == i) & (lane == j), value, growth)
    growth_ref[...] = growth[:vectors, :vectors]
    chunks = semaphore.shape[0] - 1
    copies = [pltpu.make_async_copy(growth_ref, growth_hbm, semaphore.at[chunks])]
    copies[0].start()
    at = {}
    for (i, j), value in inverse.items():
        at[i, j] = len(at)
        factors[at[i, j]] = scale * value
    mode_at = {}
    for i in range(vectors):
        for m in range(modes):
            mode_at[i, m] = len(at) + len(mode_at)
            factors[mode_at[i, m]] = -scale * sum(inverse[i, j] * coef[m, j] for j in range(i + 1))
    for f in range(fields):
        for own, x in zip(planes, layers):
            out_ref[f, pl.ds(x, depth, stride=width), :] = own[f]
    outer = (row % width == 0) | (row % width == width - 1)

    def step(k, carry):
        for c in range(comps):
            parts = []
            for v in range(vectors):
                inner = block(advanced, v * comps + c, k)
                parts.append(jnp.where(outer, block(out_ref, v * comps + c, k), inner))
            values = []
            for i in range(vectors):
                value = factors[at[i, 0]] * parts[0]
                for j in range(1, i + 1):
                    value = value + factors[at[i, j]] * parts[j]
                values.append(value)
            for m in range(modes):
                mode = block(dual, m * comps + c, k)
                for i in range(vectors):
                    values[i] = values[i] + factors[mode_at[i, m]] * mode
            for i in range(vectors):
                put_block(out_ref, i * comps + c, k, values[i])
        return carry

    size = rows_all // SUB // chunks
    for n in range(chunks):
        lax.fori_loop(n * size, (n + 1) * size, step, 0)
        rows = pl.ds(n * size * SUB, size * SUB)
        copy = pltpu.make_async_copy(out_ref.at[:, rows], out_hbm.at[:, rows], semaphore.at[n])
        copy.start()
        copies.append(copy)
    for copy in copies:
        copy.wait()


def swap(first, second, axis):
    count = lax.axis_size(axis)
    results = []
    for field, start in ((first, 0), (second, 1)):
        pairs = [(i, i + 1) for i in range(start, count - 1, 2)]
        results.append(lax.ppermute(field, axis, pairs + [(j, i) for i, j in pairs]))
    return results


def exchange(payload):
    return lax.all_to_all(payload, ("gx", "gy"), 0, 0, tiled=True)


def body(adjoint_block, base_flow, direct_modes, dual_modes):
    vectors, comps, depth, width, length = adjoint_block.shape
    steps, modes = base_flow.shape[0], direct_modes.shape[0]
    rows = depth * width
    assert length == LANES and SUB % width == 0 and rows % SUB == 0 and depth % SUB == 0
    devices = lax.axis_size("gx") * lax.axis_size("gy")
    cells = float(comps * rows * length * devices)
    fields = vectors * comps

    q = adjoint_block.reshape(fields, rows, length)
    base = base_flow.reshape(steps * comps, rows, length)
    direct = direct_modes.reshape(modes * comps, rows, length)
    dual = dual_modes.reshape(modes * comps, rows, length)
    plane = (depth, length)

    sets = [
        [(0, f) for f in range(fields)] + [(1, j) for j in range(comps)],
        [(1, comps + j) for j in range(comps)],
    ]
    q, base, *layers, late_a, late_b = call(
        functools.partial(pack_x_kernel, width, sets),
        1.5,
        [q.shape, base.shape] + [(len(some), *plane) for some in sets for _ in range(2)],
        q,
        base,
        scratch=[pltpu.SemaphoreType.DMA((fields + steps * comps,))],
        hbm_args=(0, 1),
    )
    halo_x = swap(*layers, "gx")
    halo_y = swap(*call(pack_y_kernel, 3, [(rows, LANES)] * 2, q, base), "gy")

    pairs, mode_pairs = pairs_of(vectors), pairs_of(modes)
    first = {(m, i): m * vectors + i for m in range(modes) for i in range(vectors)}
    cross = {key: modes * vectors + lane for key, lane in first.items()}
    self_gram = {key: 2 * modes * vectors + n for n, key in enumerate(pairs)}
    slot = 2 * modes * vectors + len(pairs)
    metric = {key: slot + n for n, key in enumerate(mode_pairs)}
    assert slot + len(mode_pairs) <= LANES
    direct, dual, direct_planes, dual_planes, metric_part = call(
        functools.partial(modes_kernel, width, modes, slot),
        4,
        [direct.shape, dual.shape] + [(2, modes * comps, *plane)] * 2 + [(SUB, LANES)],
        direct,
        dual,
        scratch=[pltpu.SemaphoreType.DMA((2, modes * comps))],
        hbm_args=(0, 1),
    )

    spacing = LANES // (1 << (modes * vectors - 1).bit_length())
    spaced = [spacing * n for n in range(modes * vectors)]
    advanced, planes, sums = call(
        functools.partial(advance_kernel, width, comps, 0, fields, 1),
        5,
        [(fields, rows, length), (2, fields, *plane), (modes * vectors, SUB, LANES)],
        q,
        base,
        *halo_y,
        *halo_y,
        direct,
    )
    edge, payload = edges(
        width,
        comps,
        (fields, fields),
        spaced,
        1.5,
        devices,
        layers,
        layers,
        halo_x,
        halo_x,
        planes,
        sums,
        [direct_planes],
        [],
    )
    gathered = exchange(payload)

    scratch = [pltpu.VMEM((modes * vectors, SUB, LANES), jnp.float32)]
    layers = call(
        functools.partial(deflate_planes_kernel, comps, spaced),
        0.8,
        [(fields + comps, *plane)] * 2,
        gathered,
        *edge,
        late_a,
        late_b,
        dual_planes,
        scratch=scratch,
    )
    halo_x = swap(*layers, "gx")
    current, *columns = call(
        functools.partial(deflate_kernel, width, comps, spaced),
        3,
        [(fields, rows, length), (rows, LANES), (rows, LANES)],
        gathered,
        advanced,
        dual,
        *layers,
        scratch=scratch,
    )
    columns = swap(*columns, "gy")
    advanced, planes, sums = call(
        functools.partial(advance_kernel, width, comps, comps, fields + comps, 2),
        12,
        [(fields, rows, length), (2, fields, *plane), (2 * modes * vectors + len(pairs), SUB, LANES)],
        current,
        base,
        *columns,
        *halo_y,
        direct,
        dual,
    )
    lanes = list(first.values()) + list(cross.values()) + list(self_gram.values())
    edge, payload = edges(
        width,
        comps,
        (fields, fields),
        lanes,
        2.2,
        devices,
        layers,
        layers,
        halo_x,
        halo_x,
        planes,
        sums,
        [direct_planes, dual_planes],
        [metric_part],
    )
    total = exchange(payload)
    factor_count = vectors * (vectors + 1) // 2 + modes * vectors
    chunks = math.gcd(rows // SUB, 8)
    next_block, growth = call(
        functools.partial(finish_kernel, width, comps, (first, cross, self_gram, metric), math.sqrt(cells)),
        3,
        [(fields, rows, length), (vectors, vectors)],
        total,
        dual,
        advanced,
        *edge,
        scratch=[
            pltpu.VMEM((fields, rows, length), jnp.float32),
            pltpu.VMEM((vectors, vectors), jnp.float32),
            pltpu.VMEM((factor_count, SUB, LANES), jnp.float32),
            pltpu.SemaphoreType.DMA((chunks + 1,)),
        ],
        hbm_outs=(0, 1),
    )
    return (next_block.reshape(adjoint_block.shape), growth)


def solution(mesh):
    placed = P(None, None, None, "gx", "gy")
    return jax.shard_map(
        body,
        mesh=mesh,
        in_specs=(placed,) * 4,
        out_specs=(placed, P()),
        check_vma=False,
    )
```
